32 devices in a mesh: dp: 8 (over z, x), tensor: 4 (over y, core).
Axes of the slice: x: 2, y: 2, z: 4, core: 2. Of those that a mesh axis runs over, the one named last changes fastest.
Arguments:
- tokens: bfloat16 [3072, 768], P('dp'), may hold values from -6 to 6
- segment_ids: int32 [3072], P('dp'), may hold values from -1 to 7, as said below
- cotangent: bfloat16 [3072, 768], P('dp'), may hold values from -6 to 6
- attn_input: bfloat16 [3, 768, 768], P(None, None, 'tensor'), may hold values from -3 to 3, as said below
- query_bias: float32 [768], P('tensor'), may hold values from -3 to 3
- value_bias: float32 [768], P('tensor'), may hold values from -3 to 3
- attn_output: bfloat16 [768, 768], P('tensor'), may hold values from -2 to 2
- output_bias: float32 [768], replicated, may hold values from -2 to 2
- gain_first: float32 [768], replicated, may hold values from 0.25 to 1.75
- shift_first: float32 [768], replicated, may hold values from -2 to 2
- hidden_weight: bfloat16 [768, 3072], P(None, 'tensor'), may hold values from -0.21875 to 0.21875
- hidden_bias: float32 [3072], P('tensor'), may hold values from -3 to 3
- down_weight: bfloat16 [3072, 768], P('tensor'), may hold values from -0.109375 to 0.109375
- down_bias: float32 [768], replicated, may hold values from -2 to 2
- gain_second: float32 [768], replicated, may hold values from 0.25 to 1.75
- shift_second: float32 [768], replicated, may hold values from -2 to 2
Outputs:
- block_out: bfloat16 [3072, 768], P('dp')
- input_grad: bfloat16 [3072, 768], P('dp')
- grad_attn_input: float32 [3, 768, 768], P(None, None, 'tensor')
- grad_query_bias: float32 [768], P('tensor')
- grad_value_bias: float32 [768], P('tensor')
- grad_attn_output: float32 [768, 768], P('tensor')
- grad_output_bias: float32 [768], replicated
- grad_gain_first: float32 [768], replicated
- grad_shift_first: float32 [768], replicated
- grad_hidden_weight: float32 [768, 3072], P(None, 'tensor')
- grad_hidden_bias: float32 [3072], P('tensor')
- grad_down_weight: float32 [3072, 768], P('tensor')
- grad_down_bias: float32 [768], replicated
- grad_gain_second: float32 [768], replicated
- grad_shift_second: float32 [768], replicated
The draws below stay inside these ranges and needn't reach their ends.
Inputs may be any that keep to these rules, and one draw needn't show every extreme that they name: `segment_ids`: block g of 384 slots (the slots of one index of dp) begins with one sequence of id g, of 192 to 384 tokens; its remaining slots are padding with id -1. In every draw some block holds a sequence of 384 tokens. `attn_input`: entries of order D ** -0.5.
All inputs are finite; a program needn't handle non-finite values.
Results may differ from the reference program's by a relative error of at most 0.011.
Values sent between devices are 32-bit elements; how exact they have to be, the bound alone decides.
A program may use at most 128 MiB of HBM per device.

```python
import jax
import jax.numpy as jnp
from jax import lax

D = 768
HEADS = 12
HD = 64
FF = 3072
CAP = 384
MINSEQ = 192
TOKENS = 3072


def draw_segment_ids(key, part):
    groups = TOKENS // CAP
    key_length, key_forced = jax.random.split(jax.random.fold_in(key, 7), 2)
    lengths = jax.random.randint(key_length, (groups,), MINSEQ, CAP + 1)
    forced = jax.random.randint(key_forced, (), 0, groups)
    block_index = jnp.arange(groups)
    lengths = jnp.where(block_index == forced, CAP, lengths)
    position = jnp.arange(CAP)
    inside = position[None, :] < lengths[:, None]
    segment_table = jnp.where(inside, jnp.arange(groups, dtype=jnp.int32)[:, None], -1)
    return segment_table.reshape(TOKENS).astype(jnp.int32)


def draw_attn_input(key, part):
    base_key = jax.random.fold_in(jax.random.fold_in(key, 11), 0)
    base = jnp.clip(jax.random.normal(base_key, (3, D, D), jnp.float32), -4.0, 4.0) * D ** (-0.5)
    return base.astype(jnp.bfloat16)


def levels(stream_key, extent, shards, least, top_value):
    def one(axis_at, parts):
        steps = jax.random.uniform(jax.random.fold_in(jax.random.fold_in(stream_key, 6), axis_at), (parts,), jnp.float32, least / len(shards), top_value / len(shards))
        return jnp.repeat(jnp.exp(steps), extent[axis_at] // parts).reshape((-1,) + (1,) * (len(extent) - axis_at - 1))

    gain = one(*shards[0])
    for cut in shards[1:]:
        gain = gain * one(*cut)
    return gain


def bell_draw(stream_key, shape, scale, reach, cuts=(), kind=jnp.bfloat16):
    result = jax.random.normal(stream_key, shape, jnp.float32) * scale
    if len(cuts) > 0:
        result = levels(stream_key, shape, cuts, -0.22, 0.18) * result
    return jnp.clip(result, min=-reach, max=reach).astype(kind)


def setup_inputs(seed: int = 0) -> dict:
    splits = jax.random.split(jax.random.key(seed), 17)
    return {
        "tokens": bell_draw(splits[0], (TOKENS, D), 1.0, 6.0, ((0, 8),)),
        "segment_ids": draw_segment_ids(jax.random.fold_in(splits[16], 71), 0),
        "cotangent": bell_draw(splits[2], (TOKENS, D), 1.0, 6.0, ((0, 8),)),
        "attn_input": draw_attn_input(jax.random.fold_in(splits[16], 71), 0),
        "query_bias": bell_draw(splits[4], (D,), 0.5, 3.0, ((0, 4),), jnp.float32),
        "value_bias": bell_draw(splits[5], (D,), 0.5, 3.0, ((0, 4),), jnp.float32),
        "attn_output": bell_draw(splits[6], (D, D), (D * 4 // CAP) ** -0.5, 2.0, ((0, 4),)),
        "output_bias": bell_draw(splits[7], (D,), 0.3, 2.0, (), jnp.float32),
        "gain_first": jnp.clip(1.0 + 0.15 * jax.random.normal(splits[8], (D,), jnp.float32), 0.25, 1.75),
        "shift_first": bell_draw(splits[9], (D,), 0.3, 2.0, (), jnp.float32),
        "hidden_weight": bell_draw(splits[10], (D, FF), D ** -0.5, 0.21875, ((1, 4),)),
        "hidden_bias": bell_draw(splits[11], (FF,), 0.5, 3.0, ((0, 4),), jnp.float32),
        "down_weight": bell_draw(splits[12], (FF, D), FF ** -0.5, 0.109375, ((0, 4),)),
        "down_bias": bell_draw(splits[13], (D,), 0.3, 2.0, (), jnp.float32),
        "gain_second": jnp.clip(1.0 + 0.15 * jax.random.normal(splits[14], (D,), jnp.float32), 0.25, 1.75),
        "shift_second": bell_draw(splits[15], (D,), 0.3, 2.0, (), jnp.float32),
    }


EPSILON = 1e-05
TANH_SCALE = 0.7978845608028654
CUBIC = 0.044715

def norm_forward(values_in, norm_gain, norm_shift):
    row_mean = lax.optimization_barrier(jnp.mean(values_in, axis=-1, keepdims=True))
    centered = values_in - row_mean
    inverse = lax.rsqrt(lax.optimization_barrier(jnp.mean(centered * centered, axis=-1, keepdims=True)) + EPSILON)
    normed = centered * inverse
    return (normed, inverse, normed * norm_gain + norm_shift)

def norm_backward(grad_out, normed, inverse, norm_gain):
    scaled = grad_out * norm_gain
    return inverse * (scaled - lax.optimization_barrier(jnp.mean(scaled, axis=-1, keepdims=True)) - normed * lax.optimization_barrier(jnp.mean(scaled * normed, axis=-1, keepdims=True)))

def gelu_pair(pre_act):
    tangent = jnp.tanh(TANH_SCALE * (pre_act + CUBIC * pre_act * pre_act * pre_act))
    gelu_value = 0.5 * pre_act * (1.0 + tangent)
    gelu_slope = 0.5 * (1.0 + tangent) + 0.5 * pre_act * (1.0 - tangent * tangent) * TANH_SCALE * (1.0 + 3.0 * CUBIC * pre_act * pre_act)
    return (gelu_value, gelu_slope)

def allowed_mask(segments):
    position = jnp.arange(segments.shape[0])
    return (segments[:, None] == segments[None, :]) & (position[None, :] <= position[:, None])

def head_scores(queries, keys_bf, allowed):
    scaling = queries.shape[-1] ** (-0.5)
    scores = jnp.einsum('qhd,khd->hqk', queries.astype(jnp.float32), keys_bf.astype(jnp.float32)) * scaling
    return jnp.where(allowed[None], scores, -jnp.inf)

def attend(queries, keys_bf, values_bf, allowed):
    scores = head_scores(queries, keys_bf, allowed)
    top_score = lax.optimization_barrier(jnp.max(scores, axis=-1, keepdims=True))
    log_sum = top_score + jnp.log(lax.optimization_barrier(jnp.sum(jnp.exp(scores - top_score), axis=-1, keepdims=True)))
    probs = jnp.exp(scores - log_sum).astype(jnp.bfloat16)
    mixed = jnp.einsum('hqk,khd->qhd', probs.astype(jnp.float32), values_bf.astype(jnp.float32))
    return (mixed, log_sum)

def attend_back(queries, keys_bf, values_bf, allowed, log_sum, grad_mixed):
    probs_full = jnp.exp(head_scores(queries, keys_bf, allowed) - log_sum)
    probs_bf = probs_full.astype(jnp.bfloat16).astype(jnp.float32)
    grad_float = grad_mixed.astype(jnp.float32)
    grad_values = jnp.einsum('hqk,qhd->khd', probs_bf, grad_float)
    grad_probs = jnp.einsum('qhd,khd->hqk', grad_float, values_bf.astype(jnp.float32))
    scaling = queries.shape[-1] ** (-0.5)
    grad_scores = (probs_full * (grad_probs - lax.optimization_barrier(jnp.sum(probs_full * grad_probs, axis=-1, keepdims=True))) * scaling).astype(jnp.bfloat16).astype(jnp.float32)
    grad_queries = jnp.einsum('hqk,khd->qhd', grad_scores, keys_bf.astype(jnp.float32))
    grad_keys = jnp.einsum('hqk,qhd->khd', grad_scores, queries.astype(jnp.float32))
    return (grad_queries, grad_keys, grad_values)

def group_pass(token_block, segment_block, cot_raw, weights):
    attn_input, query_bias, value_bias, attn_output, output_bias, gain_first, shift_first, hidden_weight, hidden_bias, down_weight, down_bias, gain_second, shift_second = weights
    row_count = token_block.shape[0]
    valid = (segment_block >= 0)[:, None]
    cot_block = jnp.where(valid, cot_raw, jnp.zeros_like(cot_raw))
    allowed = allowed_mask(segment_block)
    resid_in = token_block.astype(jnp.float32)
    normed_one, inverse_one, pre_one = norm_forward(resid_in, gain_first, shift_first)
    hidden_one = pre_one.astype(jnp.bfloat16)
    queries = (jnp.dot(hidden_one, attn_input[0], preferred_element_type=jnp.float32) + query_bias).astype(jnp.bfloat16).reshape(row_count, HEADS, HD)
    keys_bf = jnp.dot(hidden_one, attn_input[1], preferred_element_type=jnp.float32).astype(jnp.bfloat16).reshape(row_count, HEADS, HD)
    values_bf = (jnp.dot(hidden_one, attn_input[2], preferred_element_type=jnp.float32) + value_bias).astype(jnp.bfloat16).reshape(row_count, HEADS, HD)
    mixed, log_sum = attend(queries, keys_bf, values_bf, allowed)
    attended = mixed.reshape(row_count, D).astype(jnp.bfloat16)
    middle = resid_in + jnp.dot(attended, attn_output, preferred_element_type=jnp.float32) + output_bias
    normed_two, inverse_two, pre_two = norm_forward(middle, gain_second, shift_second)
    hidden_two = pre_two.astype(jnp.bfloat16)
    pre_act = jnp.dot(hidden_two, hidden_weight, preferred_element_type=jnp.float32) + hidden_bias
    gelu_value, gelu_slope = gelu_pair(pre_act)
    activation = gelu_value.astype(jnp.bfloat16)
    out_full = middle + jnp.dot(activation, down_weight, preferred_element_type=jnp.float32) + down_bias
    out_block = jnp.where(valid, out_full, jnp.zeros_like(out_full)).astype(jnp.bfloat16)
    grad_top = cot_block.astype(jnp.float32)
    grad_down_bias = lax.optimization_barrier(jnp.sum(grad_top, axis=0))
    grad_down_weight = jnp.dot(activation.T, cot_block, preferred_element_type=jnp.float32)
    grad_pre = jnp.dot(cot_block, down_weight.T, preferred_element_type=jnp.float32) * gelu_slope
    grad_hidden_bias = lax.optimization_barrier(jnp.sum(grad_pre, axis=0))
    grad_pre_bf = grad_pre.astype(jnp.bfloat16)
    grad_hidden_weight = jnp.dot(hidden_two.T, grad_pre_bf, preferred_element_type=jnp.float32)
    grad_two = jnp.dot(grad_pre_bf, hidden_weight.T, preferred_element_type=jnp.float32)
    grad_gain_second = lax.optimization_barrier(jnp.sum(grad_two * normed_two, axis=0))
    grad_shift_second = lax.optimization_barrier(jnp.sum(grad_two, axis=0))
    grad_middle = grad_top + norm_backward(grad_two, normed_two, inverse_two, gain_second)
    grad_output_bias = lax.optimization_barrier(jnp.sum(grad_middle, axis=0))
    grad_middle_bf = grad_middle.astype(jnp.bfloat16)
    grad_attn_output = jnp.dot(attended.T, grad_middle_bf, preferred_element_type=jnp.float32)
    grad_attended = jnp.dot(grad_middle_bf, attn_output.T, preferred_element_type=jnp.float32).astype(jnp.bfloat16).reshape(row_count, HEADS, HD)
    grad_queries, grad_keys, grad_values = attend_back(queries, keys_bf, values_bf, allowed, log_sum, grad_attended)
    grad_queries = grad_queries.reshape(row_count, D)
    grad_keys = grad_keys.reshape(row_count, D)
    grad_values = grad_values.reshape(row_count, D)
    grad_query_bias = lax.optimization_barrier(jnp.sum(grad_queries, axis=0))
    grad_value_bias = lax.optimization_barrier(jnp.sum(grad_values, axis=0))
    query_bf = grad_queries.astype(jnp.bfloat16)
    key_grad_bf = grad_keys.astype(jnp.bfloat16)
    value_grad_bf = grad_values.astype(jnp.bfloat16)
    grad_attn_input = jnp.stack([jnp.dot(hidden_one.T, query_bf, preferred_element_type=jnp.float32), jnp.dot(hidden_one.T, key_grad_bf, preferred_element_type=jnp.float32), jnp.dot(hidden_one.T, value_grad_bf, preferred_element_type=jnp.float32)])
    grad_one = jnp.dot(query_bf, attn_input[0].T, preferred_element_type=jnp.float32) + jnp.dot(key_grad_bf, attn_input[1].T, preferred_element_type=jnp.float32) + jnp.dot(value_grad_bf, attn_input[2].T, preferred_element_type=jnp.float32)
    grad_gain_first = lax.optimization_barrier(jnp.sum(grad_one * normed_one, axis=0))
    grad_shift_first = lax.optimization_barrier(jnp.sum(grad_one, axis=0))
    grad_block = (grad_middle + norm_backward(grad_one, normed_one, inverse_one, gain_first)).astype(jnp.bfloat16)
    grads = (grad_attn_input, grad_query_bias, grad_value_bias, grad_attn_output, grad_output_bias, grad_gain_first, grad_shift_first, grad_hidden_weight, grad_hidden_bias, grad_down_weight, grad_down_bias, grad_gain_second, grad_shift_second)
    return (out_block, grad_block, grads)

def add_terms(left_term, right_term):
    return left_term + right_term

def reference(tokens, segment_ids, cotangent, attn_input, query_bias, value_bias, attn_output, output_bias, gain_first, shift_first, hidden_weight, hidden_bias, down_weight, down_bias, gain_second, shift_second):
    groups = TOKENS // CAP
    weights = (attn_input, query_bias, value_bias, attn_output, output_bias, gain_first, shift_first, hidden_weight, hidden_bias, down_weight, down_bias, gain_second, shift_second)
    shapes = [(3, D, D), (D,), (D,), (D, D), (D,), (D,), (D,), (D, FF), (FF,), (FF, D), (D,), (D,), (D,)]
    initial = tuple((jnp.zeros(shape_item, jnp.float32) for shape_item in shapes))

    def one_group(totals, block):
        token_block, segment_block, cot_block = block
        out_block, grad_block, grads = group_pass(token_block, segment_block, cot_block, weights)
        return (jax.tree.map(add_terms, totals, grads), (out_block, grad_block))
    blocks = (tokens.reshape(groups, CAP, D), segment_ids.reshape(groups, CAP), cotangent.reshape(groups, CAP, D))
    totals, outputs = lax.scan(one_group, initial, blocks)
    block_out = outputs[0].reshape(TOKENS, D)
    input_grad = outputs[1].reshape(TOKENS, D)
    return (block_out, input_grad, totals[0], totals[1], totals[2], totals[3], totals[4], totals[5], totals[6], totals[7], totals[8], totals[9], totals[10], totals[11], totals[12])
```

```python
import types

import jax
import jax.numpy as jnp
from jax import lax
from jax.experimental import pallas as pl
from jax.experimental.pallas import tpu as pltpu
from jax.sharding import PartitionSpec as P

HD = 64
MESH = pl.DeviceIdType.MESH
VM = pl.BlockSpec(memory_space=pltpu.VMEM)


EPSILON = 1e-05
TANH_SCALE = 0.7978845608028654
CUBIC = 0.044715


def norm_forward(values_in, norm_gain, norm_shift):
    row_mean = jnp.mean(values_in, axis=-1, keepdims=True)
    centered = values_in - row_mean
    inverse = lax.rsqrt(jnp.mean(centered * centered, axis=-1, keepdims=True) + EPSILON)
    normed = centered * inverse
    return (normed, inverse, normed * norm_gain + norm_shift)


def norm_backward(grad_out, normed, inverse, norm_gain):
    scaled = grad_out * norm_gain
    return inverse * (
        scaled
        - jnp.mean(scaled, axis=-1, keepdims=True)
        - normed * jnp.mean(scaled * normed, axis=-1, keepdims=True)
    )


def gelu_pair(pre_act):
    tangent = jnp.tanh(TANH_SCALE * (pre_act + CUBIC * pre_act * pre_act * pre_act))
    gelu_value = 0.5 * pre_act * (1.0 + tangent)
    gelu_slope = 0.5 * (1.0 + tangent) + 0.5 * pre_act * (1.0 - tangent * tangent) * TANH_SCALE * (
        1.0 + 3.0 * CUBIC * pre_act * pre_act
    )
    return (gelu_value, gelu_slope)


def contract_rows(left_mat, right_mat):
    return lax.dot_general(
        left_mat, right_mat, (((0,), (0,)), ((), ())), preferred_element_type=jnp.float32
    )


def contract_cols(left_mat, right_mat):
    return lax.dot_general(
        left_mat, right_mat, (((1,), (1,)), ((), ())), preferred_element_type=jnp.float32
    )


def allowed_mask(segments):
    position = jnp.arange(segments.shape[0])
    return (segments[:, None] == segments[None, :]) & (position[None, :] <= position[:, None])


def head_scores(queries, keys_bf, allowed):
    scaling = queries.shape[-1] ** (-0.5)
    scores = (
        jnp.einsum("qhd,khd->hqk", queries, keys_bf, preferred_element_type=jnp.float32) * scaling
    )
    return jnp.where(allowed[None], scores, -jnp.inf)


def attend(queries, keys_bf, values_bf, allowed):
    scores = head_scores(queries, keys_bf, allowed)
    top_score = jnp.max(scores, axis=-1, keepdims=True)
    log_sum = top_score + jnp.log(jnp.sum(jnp.exp(scores - top_score), axis=-1, keepdims=True))
    probs = jnp.exp(scores - log_sum).astype(jnp.bfloat16)
    mixed = jnp.einsum("hqk,khd->qhd", probs, values_bf, preferred_element_type=jnp.float32)
    return (mixed, log_sum)


def attend_back(queries, keys_bf, values_bf, allowed, log_sum, grad_mixed):
    probs_full = jnp.exp(head_scores(queries, keys_bf, allowed) - log_sum)
    probs_bf = probs_full.astype(jnp.bfloat16)
    grad_values = jnp.einsum(
        "hqk,qhd->khd", probs_bf, grad_mixed, preferred_element_type=jnp.float32
    )
    grad_probs = jnp.einsum(
        "qhd,khd->hqk", grad_mixed, values_bf, preferred_element_type=jnp.float32
    )
    scaling = queries.shape[-1] ** (-0.5)
    grad_scores = (
        probs_full
        * (grad_probs - jnp.sum(probs_full * grad_probs, axis=-1, keepdims=True))
        * scaling
    ).astype(jnp.bfloat16)
    grad_queries = jnp.einsum(
        "hqk,khd->qhd", grad_scores, keys_bf, preferred_element_type=jnp.float32
    )
    grad_keys = jnp.einsum("hqk,qhd->khd", grad_scores, queries, preferred_element_type=jnp.float32)
    return (grad_queries, grad_keys, grad_values)


CHUNK = 32
BLOCK = 128
NPIECES = 12
LAG = 2
LIMIT = 67043328


def dot(left, right, left_dim, right_dim):
    return lax.dot_general(
        left, right, (((left_dim,), (right_dim,)), ((), ())), preferred_element_type=jnp.float32
    )


def remote(src, dst, send, recv, device):
    return pltpu.make_async_remote_copy(
        src_ref=src,
        dst_ref=dst,
        send_sem=send,
        recv_sem=recv,
        device_id=device,
        device_id_type=MESH,
    )


def push(src, dst, send, recv, device):
    copy = remote(src, dst, send, recv, device)
    copy.start()
    return copy


def greet(peers):
    barrier = pltpu.get_barrier_semaphore()
    for peer in peers:
        pl.semaphore_signal(barrier, inc=1, device_id=peer, device_id_type=MESH)
    pl.semaphore_wait(barrier, len(peers))


class Place:
    def __init__(self):
        dp = self.dp = lax.axis_index("dp")
        me = self.me = lax.axis_index("tensor")
        x = self.x = dp % 2
        line = dp // 2
        y, k = me // 2, me % 2
        self.k = k
        self.inner = (line == 1) | (line == 2)
        self.edge = (line == 0) | (line == 3)
        odd = line % 2
        self.xn = (dp + 1 - 2 * x, me)
        self.yn = (dp, (me + 2) % 4)
        self.cn = (dp, me + 1 - 2 * k)
        self.beside = ((line + 1 - 2 * odd) * 2 + x, me)
        self.mirror = ((3 - line) * 2 + x, me)
        self.q = k * 2 + y
        self.qy = k * 2 + 1 - y
        self.qc = (1 - k) * 2 + y
        self.qcy = (1 - k) * 2 + 1 - y


class Reduce:
    def __init__(self, place, part, rx, mid, ry, send, recv):
        self.p, self.part, self.rx, self.mid, self.ry = place, part, rx, mid, ry
        self.send, self.recv = send, recv

    def start(self):
        p = self.p
        self.c = [
            push(self.part.at[p.qcy], self.rx.at[0], self.send.at[0], self.recv.at[0], p.cn),
            push(self.part.at[p.qc], self.rx.at[1], self.send.at[1], self.recv.at[1], p.cn),
        ]

    def first(self):
        p = self.p
        self.c[0].wait_recv()
        self.mid[...] = self.part[p.qy] + self.rx[0]
        self.c.append(push(self.mid, self.ry, self.send.at[2], self.recv.at[2], p.yn))

    def second(self):
        self.c[1].wait_recv()
        self.rx[1] = self.part[self.p.q] + self.rx[1]

    def wait(self):
        self.c[2].wait_recv()

    def rows(self, at, size):
        return self.rx[1, pl.ds(at, size), :] + self.ry[pl.ds(at, size), :]

    def drain(self):
        for copy in self.c:
            copy.wait_send()


class Gather:
    def __init__(self, place, own, peer, send, recv):
        self.p, self.own, self.peer, self.send, self.recv = place, own, peer, send, recv
        self.c = {}

    def go(self, n, ref, at, device, into=None):
        into = ref if into is None else into
        self.c[n] = push(ref.at[at], into.at[at], self.send.at[n], self.recv.at[n], device)

    def start(self):
        p = self.p
        self.go(0, self.own, p.q, p.yn)
        self.go(3, self.own, p.q, p.cn)
        if self.peer is not None:
            self.go(1, self.own, p.q, p.xn, self.peer)

    def from_y(self):
        self.c[0].wait_recv()
        self.go(4, self.own, self.p.qy, self.p.cn)
        if self.peer is not None:
            self.slip(7, self.own, self.p.qy, 0, self.p.xn)

    def own_done(self):
        self.c[3].wait_recv()
        self.c[4].wait_recv()

    def from_x(self):
        self.c[1].wait_recv()
        self.slip(2, self.peer, self.p.q, 1, self.p.yn)
        self.go(5, self.peer, self.p.q, self.p.cn)

    def slip(self, n, ref, at, part, device):
        size = ref.shape[1] // 2
        rows = pl.ds(part * size, size)
        src, into = ref.at[at, rows], self.peer.at[at, rows]
        self.c[n] = push(src, into, self.send.at[n], self.recv.at[n], device)

    def from_diagonal(self):
        self.c[2].wait_recv()
        self.c[7].wait_recv()
        self.go(6, self.peer, self.p.qy, self.p.cn)

    def peer_done(self):
        self.c[5].wait_recv()
        self.c[6].wait_recv()

    def drain(self):
        for copy in self.c.values():
            copy.wait_send()


class Swap:
    def __init__(self, place, src, dst, send, recv):
        self.p, self.src, self.dst, self.send, self.recv = place, src, dst, send, recv
        half = src.shape[0] // 2
        self.rows = pl.ds(pl.multiple_of(place.k * half, 8), half)

    def start(self):
        src, dst = self.src.at[self.rows], self.dst.at[self.rows]
        self.c = [push(src, dst, self.send.at[0], self.recv.at[0], self.p.xn)]

    def share(self):
        self.c[0].wait_recv()
        dst = self.dst.at[self.rows]
        self.c.append(push(dst, dst, self.send.at[1], self.recv.at[1], self.p.cn))

    def done(self):
        self.c[1].wait_recv()

    def drain(self):
        for copy in self.c:
            copy.wait_send()


def layout(operands):
    rows, width = operands[0].shape
    local, hidden = operands[3].shape[0] // 3, operands[10].shape[1]
    heads, quarter, half = local // HD, rows // 4, hidden // 2
    f32, bf16 = jnp.float32, jnp.bfloat16
    b = types.SimpleNamespace()
    b.args = [pltpu.VMEM(item.shape, item.dtype) for item in operands]
    b.arg_sem = pltpu.SemaphoreType.DMA((len(operands),))

    def mem(*shape, kind=f32):
        return pltpu.VMEM(shape, kind)

    def sems(count):
        return [pltpu.SemaphoreType.DMA((count,))] * 2

    b.tok_f, b.cot_f = mem(rows, width), mem(rows, width)
    b.tok_peer, b.cot_peer = [mem(rows, width)] * 2
    b.swaps = [sems(2)] * 2
    b.len_own, b.len_peer, b.len_sem = mem(8, 128), mem(8, 128), sems(1)
    b.hid1, b.h2, b.cots, b.gms = [mem(2 * rows, width, kind=bf16)] * 4
    b.stack = mem(2 * rows, 4 * 256, kind=bf16)
    b.acth, b.gpreh = [mem(2 * rows, half, kind=bf16)] * 2
    b.act, b.gpre = [mem(rows, hidden, kind=bf16)] * 2
    b.pre, b.gact, b.gact_peer = mem(rows, hidden), mem(rows, hidden), mem(rows, half)
    b.probs = mem(heads, rows, rows)
    b.heads = mem(3 * heads, rows, HD, kind=bf16)
    b.gk, b.gv = mem(rows, HD), mem(rows, HD)
    four, two, one = mem(4, quarter, width), mem(2, quarter, width), mem(quarter, width)
    b.sums = [[four, two, one, one, *sems(3)]] * 4
    b.wide = [[four, four, *sems(8)]] * 2
    b.slim = [[four, *sems(7)]] * 2
    b.middle, b.gmid = one, one
    b.parts = [mem(half, width), mem(width, half), mem(2 * local, width)]
    cut = [(x.shape[0] // NPIECES, x.shape[1]) for x in b.parts]
    b.rz = [mem(NPIECES, *shape) for shape in cut]
    b.ry = [mem(NPIECES, *shape) for shape in cut]
    b.tots = [mem(hidden, width), mem(width, hidden), mem(4 * local, width)]
    b.up, b.cross, b.down, b.give = [sems(3 * NPIECES)] * 4
    b.bias, b.mine = mem(8, hidden), mem(8, width)
    b.notes, b.heard, b.note_sem = mem(5, 8, width), mem(5, 8, width), sems(5)
    b.tiles, b.total = [mem(rows, width, kind=bf16)] * 2, mem(8, width)
    b.out = pltpu.SemaphoreType.DMA((7,))
    return vars(b)


def loop(rows, body, init=None, size=CHUNK):
    if init is None:

        def run(i, _):
            body(pl.multiple_of(i * size, size))
            return 0

        lax.fori_loop(0, rows // size, run, 0)
        return None
    return lax.fori_loop(0, rows // size, lambda i, c: body(pl.multiple_of(i * size, size), c), init)


def column_sum(values):
    return jnp.sum(values, axis=0, keepdims=True)


def block_kernel(tree, *refs):
    (block_out, input_grad, grad_in, grad_out, grad_hidden, grad_down) = refs[16:22]
    small_out = refs[22]
    s = types.SimpleNamespace(**jax.tree.unflatten(tree, refs[23:]))
    (tokens, cot, seg, attn_rows, query_bias, value_bias, attn_output, output_bias) = s.args[:8]
    (gain_one, shift_one, hidden_w, hidden_bias, down_w, down_bias, gain_two, shift_two) = s.args[8:]
    loads = [pltpu.make_async_copy(refs[n], s.args[n], s.arg_sem.at[n]) for n in range(16)]
    for n in (2, 1, 0, 8, 9, 3, 4, 5, 6, 7, 14, 15, 12, 10, 11, 13):
        loads[n].start()

    def ready(*which):
        for n in which:
            loads[n].wait()
    f32, bf16 = jnp.float32, jnp.bfloat16
    rows, width = tokens.shape
    local = attn_rows.shape[0] // 3
    hidden = hidden_w.shape[1]
    heads, quarter, half = local // HD, rows // 4, hidden // 2
    p = Place()

    def line(ref):
        return ref[...].reshape(1, ref.shape[0])

    sum1, sum2, sum3, sum4 = (Reduce(p, *item) for item in s.sums)
    all1, all2 = (Gather(p, *item) for item in s.wide)
    all3, all4 = (Gather(p, own, None, *rest) for own, *rest in s.slim)
    swap_cot = Swap(p, s.cot_f, s.cot_peer, *s.swaps[0])
    swap_tok = Swap(p, s.tok_f, s.tok_peer, *s.swaps[1])

    parts, rz, ry, tots = s.parts, s.rz, s.ry, s.tots
    units = [(m, i) for m in range(3) for i in range(NPIECES)]
    count = len(units)

    def piece(u):
        m, i = units[u]
        size = parts[m].shape[0] // NPIECES
        return parts[m].at[pl.ds(i * size, size)]

    def place_of(u, column):
        m, i = units[u]
        tall, wide = parts[m].shape
        size = tall // NPIECES
        if m == 1:
            return tots[m].at[pl.ds(i * size, size), pl.ds(pl.multiple_of(column * wide, 128), wide)]
        return tots[m].at[pl.ds(pl.multiple_of(column * tall + i * size, 8), size)]

    def hop(sem, src, dst, u, device):
        return remote(src, dst, sem[0].at[u], sem[1].at[u], device)

    def up(u):
        m, i = units[u]
        return hop(s.up, piece(u), rz[m].at[i], u, p.beside)

    def cross(u):
        m, i = units[u]
        return hop(s.cross, piece(u), ry[m].at[i], u, p.mirror)

    def down(u):
        return hop(s.down, place_of(u, p.x), place_of(u, p.x), u, p.beside)

    def give(u):
        return hop(s.give, place_of(u, p.x), place_of(u, p.x), u, p.xn)

    def send_up(us):
        @pl.when(p.edge)
        def _():
            for u in us:
                up(u).start()

    def step(at):
        @pl.when(p.inner)
        def _():
            if at < count:
                m, i = units[at]
                up(at).wait_recv()
                src = piece(at)
                src[...] = src[...] + rz[m][i]
                cross(at).start()
            if 0 <= at - LAG < count:
                u = at - LAG
                m, i = units[u]
                cross(u).wait_recv()
                place_of(u, p.x)[...] = piece(u)[...] + ry[m][i]
                down(u).start()
                give(u).start()

        if 0 <= at - 2 * LAG < count:

            @pl.when(p.edge)
            def _():
                down(at - 2 * LAG).wait_recv()
                give(at - 2 * LAG).start()

    at, sent = [0], [0]

    def pump(n=1):
        for _ in range(n):
            if at[0] < sent[0] or sent[0] == count:
                step(at[0])
                at[0] += 1

    greet([p.xn, p.yn, p.cn, p.beside, p.mirror])
    copies = []

    def emit(src, ref):
        copies.append(pltpu.make_async_copy(src, ref, s.out.at[len(copies)]))
        copies[-1].start()

    ready(1, 2)
    inside = jnp.where(line(seg) >= 0, 1.0, 0.0)
    length = jnp.sum(inside, axis=1, keepdims=True)
    s.len_own[...] = jnp.broadcast_to(length, (8, 128))
    note = push(s.len_own, s.len_peer, s.len_sem[0].at[0], s.len_sem[1].at[0], p.xn)

    def row_index(at, size):
        return (lax.broadcasted_iota(jnp.int32, (size, 1), 0) + at).astype(f32)

    def mask_cot(at, total):
        r = pl.ds(at, CHUNK)
        c = jnp.where(row_index(at, CHUNK) < length, cot[r, :].astype(f32), 0.0)
        s.cot_f[r, :] = c
        s.cots[r, :] = c.astype(bf16)
        return total + column_sum(c)

    s.mine[...] = jnp.zeros_like(s.mine)
    s.mine[1:2, :] = loop(rows, mask_cot, jnp.zeros((1, width), f32))
    swap_cot.start()
    ready(0, 8, 9)
    gain1, shift1 = line(gain_one), line(shift_one)

    def first_norm(at):
        t = tokens[pl.ds(at, CHUNK), :].astype(f32)
        s.tok_f[pl.ds(at, CHUNK), :] = t
        s.hid1[pl.ds(at, CHUNK), :] = norm_forward(t, gain1, shift1)[2].astype(bf16)

    loop(rows, first_norm)

    def project(base):
        normal = s.hid1[base : base + rows, :]
        for m in range(3):
            out = dot(normal, attn_rows[m * local : (m + 1) * local, :], 1, 1)
            if m == 0:
                out = (out + line(query_bias)).astype(bf16) * jnp.asarray(HD ** (-0.5), bf16)
            elif m == 1:
                out = out.astype(bf16)
            else:
                out = (out + line(value_bias)).astype(bf16)
            for h in range(heads):
                s.heads[m * heads + h] = out[:, h * HD : (h + 1) * HD]

    def probabilities(h, i, bound):
        top_row, n = i * BLOCK, (i + 1) * BLOCK
        query = s.heads[h, top_row:n, :]
        key = s.heads[heads + h, 0:n, :]
        row = (lax.broadcasted_iota(jnp.int32, (BLOCK, n), 0) + top_row).astype(f32)
        col = lax.broadcasted_iota(jnp.int32, (BLOCK, n), 1).astype(f32)
        allowed = (col <= row) & ((col >= bound) | (row < bound))
        scores = jnp.where(allowed, dot(query, key, 1, 1), -jnp.inf)
        e = jnp.exp(scores - jnp.max(scores, axis=1, keepdims=True))
        return e * (1.0 / jnp.sum(e, axis=1, keepdims=True))

    def mix(h, i, base, probs_bf):
        n = (i + 1) * BLOCK
        value = s.heads[2 * heads + h, 0:n, :]
        mixed = dot(probs_bf, value, 1, 0).astype(bf16)
        at = 3 * 256 + h * HD
        s.stack[base + i * BLOCK : base + n, at : at + HD] = mixed

    def head_back(h, base, get, beats):
        blocks = rows // BLOCK
        for i in reversed(range(blocks)):
            if i in beats:
                pump()
            top_row, n = i * BLOCK, (i + 1) * BLOCK
            r = slice(base + top_row, base + n)
            probs = get(i)
            probs_bf = probs.astype(bf16)
            if base:
                mix(h, i, base, probs_bf)
            mixed = dot(s.gms[r, :], attn_output[h * HD : (h + 1) * HD, :], 1, 1).astype(bf16)
            value = s.heads[2 * heads + h, 0:n, :]
            key = s.heads[heads + h, 0:n, :]
            grad_probs = dot(mixed, value, 1, 1)
            weighted = jnp.sum(probs * grad_probs, axis=1, keepdims=True)
            scores = (probs * (grad_probs - weighted)).astype(bf16)
            query = s.heads[h, top_row:n, :]
            grad_query = dot(scores, key, 1, 0) * HD ** (-0.5)
            grad_key = dot(scores, query, 0, 0)
            grad_value = dot(probs_bf, mixed, 0, 0)
            s.stack[r, h * HD : (h + 1) * HD] = grad_query.astype(bf16)
            if i == blocks - 1:
                query_sum = column_sum(grad_query)
                s.gk[...] = grad_key
                s.gv[...] = grad_value
            else:
                query_sum = query_sum + column_sum(grad_query)
                s.gk[0:n, :] += grad_key
                s.gv[0:n, :] += grad_value
        s.stack[base : base + rows, 256 + h * HD : 256 + (h + 1) * HD] = s.gk[...].astype(bf16)
        s.stack[base : base + rows, 512 + h * HD : 512 + (h + 1) * HD] = s.gv[...].astype(bf16)
        if not base:
            s.mine[2:3, h * HD : (h + 1) * HD] = query_sum
            s.mine[2:3, 256 + h * HD : 256 + (h + 1) * HD] = column_sum(s.gv[...])

    ready(3, 4, 5)
    project(0)
    ready(6)
    for h in range(heads):
        for i in range(rows // BLOCK):
            n = (i + 1) * BLOCK
            probs = probabilities(h, i, length)
            s.probs[h, i * BLOCK : n, 0:n] = probs
            mix(h, i, 0, probs.astype(bf16))
    attended = s.stack[0:rows, 3 * 256 : 3 * 256 + local]
    s.sums[0][0][...] = dot(attended, attn_output[...], 1, 0).reshape(4, quarter, width)
    sum1.start()
    sum1.first()
    sum1.second()
    ready(7, 14, 15, 12)
    gain2, shift2 = line(gain_two), line(shift_two)
    s.gact[...] = dot(s.cots[0:rows, :], down_w[...], 1, 1)

    own_rows = p.q * quarter
    out_bias = line(output_bias)
    sum1.wait()

    def second_norm(at):
        r = pl.ds(pl.multiple_of(own_rows + at, CHUNK), CHUNK)
        middle = s.tok_f[r, :] + sum1.rows(at, CHUNK) + out_bias
        s.middle[pl.ds(at, CHUNK), :] = middle
        normal = norm_forward(middle, gain2, shift2)[2].astype(bf16)
        s.wide[0][0][p.q, pl.ds(at, CHUNK), :] = normal.astype(f32)

    loop(quarter, second_norm)
    all1.start()
    ready(10, 11, 13)
    cut = pl.ds(pl.multiple_of(p.x * half, 128), half)
    all1.from_y()
    all1.from_x()
    swap_tok.start()
    all1.own_done()

    s.h2[0:rows, :] = s.wide[0][0][...].reshape(rows, width).astype(bf16)
    s.pre[...] = dot(s.h2[0:rows, :], hidden_w[...], 1, 0)
    bias = line(hidden_bias)

    def activate(at, total):
        r = pl.ds(at, CHUNK)
        value, slope = gelu_pair(s.pre[r, :] + bias)
        s.act[r, :] = value.astype(bf16)
        grad = s.gact[r, :] * slope
        s.gpre[r, :] = grad.astype(bf16)
        return total + column_sum(grad)

    s.mine[0:1, :] = loop(rows, activate, jnp.zeros((1, hidden), f32))
    s.sums[1][0][...] = dot(s.gpre[...], hidden_w[...], 1, 1).reshape(4, quarter, width)
    sum2.start()
    s.sums[2][0][...] = dot(s.act[...], down_w[...], 1, 0).reshape(4, quarter, width)
    sum2.first()
    sum2.second()
    sum3.start()
    s.acth[0:rows, :] = s.act[:, cut]
    s.gpreh[0:rows, :] = s.gpre[:, cut]

    swap_cot.share()
    swap_cot.done()
    s.cots[rows:, :] = s.cot_peer[...].astype(bf16)
    s.gact_peer[...] = dot(s.cots[rows:, :], down_w[cut, :], 1, 1)
    all1.from_diagonal()
    all1.peer_done()
    s.h2[rows:, :] = s.wide[0][1][...].reshape(rows, width).astype(bf16)
    s.pre[:, 0:half] = dot(s.h2[rows:, :], hidden_w[:, cut], 1, 0)
    s.bias[0:1, :] = bias
    bias_half = s.bias[0:1, cut]

    def activate_peer(at):
        r = pl.ds(at, CHUNK)
        low = pl.ds(pl.multiple_of(rows + at, CHUNK), CHUNK)
        value, slope = gelu_pair(s.pre[r, 0:half] + bias_half)
        s.acth[low, :] = value.astype(bf16)
        s.gpreh[low, :] = (s.gact_peer[r, :] * slope).astype(bf16)

    loop(rows, activate_peer)
    parts[0][...] = dot(s.acth[...], s.cots[...], 0, 0)
    send_up(range(NPIECES))
    sent[0] = NPIECES
    parts[1][...] = dot(s.h2[...], s.gpreh[...], 0, 0)
    send_up(range(NPIECES, 2 * NPIECES))
    sent[0] = 2 * NPIECES

    sum2.wait()

    def second_back(at, total):
        r = pl.ds(pl.multiple_of(own_rows + at, CHUNK), CHUNK)
        grad = sum2.rows(at, CHUNK)
        normed, inverse, _ = norm_forward(s.middle[pl.ds(at, CHUNK), :], gain2, shift2)
        mid = s.cot_f[r, :] + norm_backward(grad, normed, inverse, gain2)
        s.gmid[pl.ds(at, CHUNK), :] = mid
        s.wide[1][0][p.q, pl.ds(at, CHUNK), :] = mid.astype(bf16).astype(f32)
        terms = (grad * normed, grad, mid)
        return tuple(t + column_sum(v) for t, v in zip(total, terms))

    sums = loop(quarter, second_back, (jnp.zeros((1, width), f32),) * 3)
    for n, value in enumerate(sums):
        s.mine[3 + n : 4 + n, :] = value
    all2.start()
    pump(3)
    all2.from_y()
    all2.from_x()
    pump()
    all2.own_done()
    s.gms[0:rows, :] = s.wide[1][0][...].reshape(rows, width).astype(bf16)
    sum3.first()
    sum3.second()
    for h in range(heads):
        get = lambda i: s.probs[h, i * BLOCK : (i + 1) * BLOCK, 0 : (i + 1) * BLOCK]
        head_back(h, 0, get, (2, 0) if h == 1 else (1,))
    pump()
    one = dot(s.stack[0:rows, 0:local], attn_rows[0:local, :], 1, 0)
    for m in range(1, 3):
        item = s.stack[0:rows, m * 256 : m * 256 + local]
        one = one + dot(item, attn_rows[m * local : (m + 1) * local, :], 1, 0)
    s.sums[3][0][...] = one.reshape(4, quarter, width)
    sum4.start()
    pump()
    sum4.first()
    sum4.second()
    swap_tok.share()
    all2.from_diagonal()
    pump()
    swap_tok.done()

    def peer_norm(at):
        low = pl.ds(pl.multiple_of(rows + at, CHUNK), CHUNK)
        t = s.tok_peer[pl.ds(at, CHUNK), :]
        s.hid1[low, :] = norm_forward(t, gain1, shift1)[2].astype(bf16)

    loop(rows, peer_norm)
    pump()
    project(rows)
    pump()
    all2.peer_done()
    s.gms[rows:, :] = s.wide[1][1][...].reshape(rows, width).astype(bf16)
    note.wait_recv()
    length_peer = s.len_peer[0:1, 0:1]
    for h in range(heads):
        head_back(h, rows, lambda i: probabilities(h, i, length_peer), (1, 0))
    pump()

    left = s.stack[:, pl.ds(pl.multiple_of(p.x * 512, 128), local)]
    parts[2][0:local, :] = dot(left, s.hid1[...], 0, 0)

    @pl.when(p.x == 0)
    def _():
        parts[2][local:, :] = dot(s.stack[:, 256 : 256 + local], s.hid1[...], 0, 0)

    @pl.when(p.x == 1)
    def _():
        parts[2][local:, :] = dot(s.stack[:, 768 : 768 + local], s.gms[...], 0, 0)

    send_up(range(2 * NPIECES, count))
    sent[0] = count
    pump()
    sum4.wait()

    def first_back(row, total):
        r = pl.ds(pl.multiple_of(own_rows + row, CHUNK), CHUNK)
        grad = sum4.rows(row, CHUNK)
        normed, inverse, _ = norm_forward(s.tok_f[r, :], gain1, shift1)
        back = norm_backward(grad, normed, inverse, gain1)
        s.slim[1][0][p.q, pl.ds(row, CHUNK), :] = s.gmid[pl.ds(row, CHUNK), :] + back
        return tuple(t + column_sum(v) for t, v in zip(total, (grad * normed, grad)))

    sums = loop(quarter, first_back, (jnp.zeros((1, width), f32),) * 2)
    for n, value in enumerate(sums):
        s.mine[6 + n : 7 + n, :] = value
    all4.start()
    notes = []

    def note_out(value, device):
        n = len(notes)
        s.notes[n] = value
        notes.append(push(s.notes.at[n], s.heard.at[n], s.note_sem[0].at[n], s.note_sem[1].at[n], device))

    def note_in():
        notes[-1].wait_recv()
        return s.notes[len(notes) - 1] + s.heard[len(notes) - 1]

    note_out(s.mine[...], p.cn)
    pump()
    sum3.wait()
    bias = line(down_bias)

    def finish_block(row):
        full = s.middle[pl.ds(row, CHUNK), :] + sum3.rows(row, CHUNK) + bias
        valid = row_index(own_rows + row, CHUNK) < length
        s.slim[0][0][p.q, pl.ds(row, CHUNK), :] = jnp.where(valid, full, 0.0)

    loop(quarter, finish_block)
    all3.start()
    pump()
    note_out(note_in(), p.yn)
    pump(2)
    all4.from_y()
    all4.own_done()
    s.tiles[1][...] = s.slim[1][0][...].reshape(rows, width).astype(bf16)
    emit(s.tiles[1], input_grad)
    which = lax.broadcasted_iota(jnp.int32, (8, width), 0)
    note_out(jnp.where(which < 3, s.mine[...], note_in()), p.xn)
    pump(2)
    all3.from_y()
    all3.own_done()
    s.tiles[0][...] = s.slim[0][0][...].reshape(rows, width).astype(bf16)
    emit(s.tiles[0], block_out)
    note_out(note_in(), p.beside)
    pump(2)
    note_out(note_in(), p.mirror)
    pump(3)
    s.total[...] = note_in()
    emit(s.total, small_out)

    def finish(m, targets):
        for u in range(m * NPIECES, (m + 1) * NPIECES):
            give(u).wait_recv()
        for start, ref in targets:
            emit(tots[m].at[pl.ds(start, ref.shape[0])], ref)

    copied = []
    while at[0] < count + 2 * LAG:
        if at[0] >= count - 2 and not copied:
            finish(0, [(0, grad_down)])
            copied.append(0)
        pump()
    if not copied:
        finish(0, [(0, grad_down)])
    finish(1, [(0, grad_hidden)])
    finish(2, [(0, grad_in), (3 * local, grad_out)])
    for job in (sum1, sum2, sum3, sum4, all1, all2, all3, all4, swap_cot, swap_tok):
        job.drain()
    for copy in [note] + notes:
        copy.wait_send()
    for u in range(count):
        give(u).wait_send()

    @pl.when(p.edge)
    def _():
        for u in range(count):
            up(u).wait_send()

    @pl.when(p.inner)
    def _():
        for u in range(count):
            cross(u).wait_send()
            down(u).wait_send()

    for copy in copies:
        copy.wait()


def emit_kernel(*refs):
    big, small, outs, vecs = refs[:6], refs[6], refs[7:13], refs[13:22]
    held, sem_in, sem_out = refs[22:28], refs[28], refs[29]
    order = (5, 4, 2, 3, 0, 1)
    reads = {n: pltpu.make_async_copy(big[n], held[n], sem_in.at[n]) for n in order}
    writes = {n: pltpu.make_async_copy(held[n], outs[n], sem_out.at[n]) for n in order}
    for n in order:
        reads[n].start()
    places = [(2, 0), (2, 256), (5, 0), (6, 0), (7, 0), (0, 0), (1, 0), (3, 0), (4, 0)]
    for ref, (row, lane) in zip(vecs, places):
        size = ref.shape[0]
        ref[...] = small[row : row + 1, lane : lane + size].reshape(size)
    for n in order:
        reads[n].wait()
        writes[n].start()
    for n in order:
        writes[n].wait()


def whole_block(operands):
    rows, width = operands[0].shape
    local = operands[3].shape[0] // 3
    hidden = operands[10].shape[1]
    f32 = jnp.float32
    scratch, tree = jax.tree.flatten(layout(operands))
    tile = jax.ShapeDtypeStruct((rows, width), jnp.bfloat16)
    mats = [(3 * local, width), (local, width), (width, hidden), (hidden, width)]
    vecs = [local, local, width, width, width, hidden, width, width, width]
    big = [tile, tile] + [jax.ShapeDtypeStruct(shape, f32) for shape in mats]
    anywhere = pl.BlockSpec(memory_space=pl.ANY)
    results = pl.pallas_call(
        lambda *refs: block_kernel(tree, *refs),
        out_shape=big + [jax.ShapeDtypeStruct((8, width), f32)],
        in_specs=[anywhere] * len(operands),
        out_specs=[anywhere] * 7,
        scratch_shapes=scratch,
        compiler_params=pltpu.CompilerParams(
            collective_id=0, has_side_effects=True, vmem_limit_bytes=LIMIT
        ),
        name="whole_block",
    )(*operands)
    return pl.pallas_call(
        emit_kernel,
        out_shape=big + [jax.ShapeDtypeStruct((n,), f32) for n in vecs],
        in_specs=[anywhere] * 6 + [VM],
        out_specs=[anywhere] * 6 + [VM] * 9,
        scratch_shapes=[pltpu.VMEM(item.shape, item.dtype) for item in big]
        + [pltpu.SemaphoreType.DMA((6,))] * 2,
        compiler_params=pltpu.CompilerParams(vmem_limit_bytes=LIMIT),
        name="emit",
    )(*results)


def plain_shards(
    tokens,
    segment_ids,
    cotangent,
    attn_input,
    query_bias,
    value_bias,
    attn_output,
    output_bias,
    gain_first,
    shift_first,
    hidden_weight,
    hidden_bias,
    down_weight,
    down_bias,
    gain_second,
    shift_second,
):
    row_count = tokens.shape[0]
    local_width = attn_input.shape[2]
    valid = (segment_ids >= 0)[:, None]
    cot_masked = jnp.where(valid, cotangent, jnp.zeros_like(cotangent))
    allowed = allowed_mask(segment_ids)
    resid_in = tokens.astype(jnp.float32)
    normed_one, inverse_one, pre_one = norm_forward(resid_in, gain_first, shift_first)
    hidden_one = pre_one.astype(jnp.bfloat16)
    projected = jnp.einsum(
        "rd,tdc->trc", hidden_one, attn_input, preferred_element_type=jnp.float32
    )
    queries = (projected[0] + query_bias).astype(jnp.bfloat16).reshape(row_count, -1, HD)
    keys_bf = projected[1].astype(jnp.bfloat16).reshape(row_count, -1, HD)
    values_bf = (projected[2] + value_bias).astype(jnp.bfloat16).reshape(row_count, -1, HD)
    mixed, log_sum = attend(queries, keys_bf, values_bf, allowed)
    attended = mixed.reshape(row_count, local_width).astype(jnp.bfloat16)
    attn_part = jnp.dot(attended, attn_output, preferred_element_type=jnp.float32)
    middle = resid_in + lax.psum(attn_part, "tensor") + output_bias
    normed_two, inverse_two, pre_two = norm_forward(middle, gain_second, shift_second)
    hidden_two = pre_two.astype(jnp.bfloat16)
    pre_act = jnp.dot(hidden_two, hidden_weight, preferred_element_type=jnp.float32) + hidden_bias
    gelu_value, gelu_slope = gelu_pair(pre_act)
    activation = gelu_value.astype(jnp.bfloat16)
    mlp_part = jnp.dot(activation, down_weight, preferred_element_type=jnp.float32)
    out_full = middle + lax.psum(mlp_part, "tensor") + down_bias
    block_out = jnp.where(valid, out_full, jnp.zeros_like(out_full)).astype(jnp.bfloat16)
    grad_top = cot_masked.astype(jnp.float32)
    grad_down_bias = jnp.sum(grad_top, axis=0)
    grad_down_weight = contract_rows(activation, cot_masked)
    grad_pre = contract_cols(cot_masked, down_weight) * gelu_slope
    grad_hidden_bias = jnp.sum(grad_pre, axis=0)
    grad_pre_bf = grad_pre.astype(jnp.bfloat16)
    grad_hidden_weight = contract_rows(hidden_two, grad_pre_bf)
    grad_two = lax.psum(contract_cols(grad_pre_bf, hidden_weight), "tensor")
    grad_gain_second = jnp.sum(grad_two * normed_two, axis=0)
    grad_shift_second = jnp.sum(grad_two, axis=0)
    grad_middle = grad_top + norm_backward(grad_two, normed_two, inverse_two, gain_second)
    grad_output_bias = jnp.sum(grad_middle, axis=0)
    grad_middle_bf = grad_middle.astype(jnp.bfloat16)
    grad_attn_output = contract_rows(attended, grad_middle_bf)
    grad_attended = (
        contract_cols(grad_middle_bf, attn_output).astype(jnp.bfloat16).reshape(row_count, -1, HD)
    )
    grad_queries, grad_keys, grad_values = attend_back(
        queries, keys_bf, values_bf, allowed, log_sum, grad_attended
    )
    grad_queries = grad_queries.reshape(row_count, local_width)
    grad_keys = grad_keys.reshape(row_count, local_width)
    grad_values = grad_values.reshape(row_count, local_width)
    grad_query_bias = jnp.sum(grad_queries, axis=0)
    grad_value_bias = jnp.sum(grad_values, axis=0)
    grad_stack = jnp.stack([grad_queries, grad_keys, grad_values]).astype(jnp.bfloat16)
    grad_attn_input = jnp.einsum(
        "rd,trc->tdc", hidden_one, grad_stack, preferred_element_type=jnp.float32
    )
    one_part = jnp.einsum("trc,tdc->rd", grad_stack, attn_input, preferred_element_type=jnp.float32)
    grad_one = lax.psum(one_part, "tensor")
    grad_gain_first = jnp.sum(grad_one * normed_one, axis=0)
    grad_shift_first = jnp.sum(grad_one, axis=0)
    input_grad = (
        grad_middle + norm_backward(grad_one, normed_one, inverse_one, gain_first)
    ).astype(jnp.bfloat16)
    (
        grad_attn_input,
        grad_query_bias,
        grad_value_bias,
        grad_attn_output,
        grad_output_bias,
        grad_gain_first,
        grad_shift_first,
        grad_hidden_weight,
        grad_hidden_bias,
        grad_down_weight,
        grad_down_bias,
        grad_gain_second,
        grad_shift_second,
    ) = lax.psum(
        (
            grad_attn_input,
            grad_query_bias,
            grad_value_bias,
            grad_attn_output,
            grad_output_bias,
            grad_gain_first,
            grad_shift_first,
            grad_hidden_weight,
            grad_hidden_bias,
            grad_down_weight,
            grad_down_bias,
            grad_gain_second,
            grad_shift_second,
        ),
        "dp",
    )
    return (
        block_out,
        input_grad,
        grad_attn_input,
        grad_query_bias,
        grad_value_bias,
        grad_attn_output,
        grad_output_bias,
        grad_gain_first,
        grad_shift_first,
        grad_hidden_weight,
        grad_hidden_bias,
        grad_down_weight,
        grad_down_bias,
        grad_gain_second,
        grad_shift_second,
    )


def shards(
    tokens,
    segment_ids,
    cotangent,
    attn_input,
    query_bias,
    value_bias,
    attn_output,
    output_bias,
    gain_first,
    shift_first,
    hidden_weight,
    hidden_bias,
    down_weight,
    down_bias,
    gain_second,
    shift_second,
):
    if lax.axis_size("tensor") != 4 or lax.axis_size("dp") != 8:
        return plain_shards(
            tokens,
            segment_ids,
            cotangent,
            attn_input,
            query_bias,
            value_bias,
            attn_output,
            output_bias,
            gain_first,
            shift_first,
            hidden_weight,
            hidden_bias,
            down_weight,
            down_bias,
            gain_second,
            shift_second,
        )
    local_width = attn_input.shape[2]
    width = tokens.shape[1]
    operands = (
        tokens,
        cotangent,
        segment_ids,
        attn_input.transpose(0, 2, 1).reshape(3 * local_width, width),
        query_bias,
        value_bias,
        attn_output,
        output_bias,
        gain_first,
        shift_first,
        hidden_weight,
        hidden_bias,
        down_weight,
        down_bias,
        gain_second,
        shift_second,
    )
    (
        block_out,
        input_grad,
        grad_in,
        grad_attn_output,
        grad_hidden_weight,
        grad_down_weight,
        grad_query_bias,
        grad_value_bias,
        grad_output_bias,
        grad_gain_first,
        grad_shift_first,
        grad_hidden_bias,
        grad_down_bias,
        grad_gain_second,
        grad_shift_second,
    ) = whole_block(operands)
    return (
        block_out,
        input_grad,
        grad_in.reshape(3, local_width, width).transpose(0, 2, 1),
        grad_query_bias,
        grad_value_bias,
        grad_attn_output,
        grad_output_bias,
        grad_gain_first,
        grad_shift_first,
        grad_hidden_weight,
        grad_hidden_bias,
        grad_down_weight,
        grad_down_bias,
        grad_gain_second,
        grad_shift_second,
    )


def solution(mesh):
    return jax.shard_map(
        shards,
        mesh=mesh,
        in_specs=(
            P("dp", None),
            P("dp"),
            P("dp", None),
            P(None, None, "tensor"),
            P("tensor"),
            P("tensor"),
            P("tensor", None),
            P(),
            P(),
            P(),
            P(None, "tensor"),
            P("tensor"),
            P("tensor", None),
            P(),
            P(),
            P(),
        ),
        out_specs=(
            P("dp", None),
            P("dp", None),
            P(None, None, "tensor"),
            P("tensor"),
            P("tensor"),
            P("tensor", None),
            P(),
            P(),
            P(),
            P(None, "tensor"),
            P("tensor"),
            P("tensor", None),
            P(),
            P(),
            P(),
        ),
        check_vma=False,
    )
```

```python
import types

import jax
import jax.numpy as jnp
from jax import lax
from jax.experimental import pallas as pl
from jax.experimental.pallas import tpu as pltpu
from jax.sharding import PartitionSpec as P

HD = 64
MESH = pl.DeviceIdType.MESH
VM = pl.BlockSpec(memory_space=pltpu.VMEM)


EPSILON = 1e-05
TANH_SCALE = 0.7978845608028654
CUBIC = 0.044715


def norm_forward(values_in, norm_gain, norm_shift):
    row_mean = jnp.mean(values_in, axis=-1, keepdims=True)
    centered = values_in - row_mean
    inverse = lax.rsqrt(jnp.mean(centered * centered, axis=-1, keepdims=True) + EPSILON)
    normed = centered * inverse
    return (normed, inverse, normed * norm_gain + norm_shift)


def norm_backward(grad_out, normed, inverse, norm_gain):
    scaled = grad_out * norm_gain
    return inverse * (
        scaled
        - jnp.mean(scaled, axis=-1, keepdims=True)
        - normed * jnp.mean(scaled * normed, axis=-1, keepdims=True)
    )


def gelu_pair(pre_act):
    tangent = jnp.tanh(TANH_SCALE * (pre_act + CUBIC * pre_act * pre_act * pre_act))
    gelu_value = 0.5 * pre_act * (1.0 + tangent)
    gelu_slope = 0.5 * (1.0 + tangent) + 0.5 * pre_act * (1.0 - tangent * tangent) * TANH_SCALE * (
        1.0 + 3.0 * CUBIC * pre_act * pre_act
    )
    return (gelu_value, gelu_slope)


def contract_rows(left_mat, right_mat):
    return lax.dot_general(
        left_mat, right_mat, (((0,), (0,)), ((), ())), preferred_element_type=jnp.float32
    )


def contract_cols(left_mat, right_mat):
    return lax.dot_general(
        left_mat, right_mat, (((1,), (1,)), ((), ())), preferred_element_type=jnp.float32
    )


def allowed_mask(segments):
    position = jnp.arange(segments.shape[0])
    return (segments[:, None] == segments[None, :]) & (position[None, :] <= position[:, None])


def head_scores(queries, keys_bf, allowed):
    scaling = queries.shape[-1] ** (-0.5)
    scores = (
        jnp.einsum("qhd,khd->hqk", queries, keys_bf, preferred_element_type=jnp.float32) * scaling
    )
    return jnp.where(allowed[None], scores, -jnp.inf)


def attend(queries, keys_bf, values_bf, allowed):
    scores = head_scores(queries, keys_bf, allowed)
    top_score = jnp.max(scores, axis=-1, keepdims=True)
    log_sum = top_score + jnp.log(jnp.sum(jnp.exp(scores - top_score), axis=-1, keepdims=True))
    probs = jnp.exp(scores - log_sum).astype(jnp.bfloat16)
    mixed = jnp.einsum("hqk,khd->qhd", probs, values_bf, preferred_element_type=jnp.float32)
    return (mixed, log_sum)


def attend_back(queries, keys_bf, values_bf, allowed, log_sum, grad_mixed):
    probs_full = jnp.exp(head_scores(queries, keys_bf, allowed) - log_sum)
    probs_bf = probs_full.astype(jnp.bfloat16)
    grad_values = jnp.einsum(
        "hqk,qhd->khd", probs_bf, grad_mixed, preferred_element_type=jnp.float32
    )
    grad_probs = jnp.einsum(
        "qhd,khd->hqk", grad_mixed, values_bf, preferred_element_type=jnp.float32
    )
    scaling = queries.shape[-1] ** (-0.5)
    grad_scores = (
        probs_full
        * (grad_probs - jnp.sum(probs_full * grad_probs, axis=-1, keepdims=True))
        * scaling
    ).astype(jnp.bfloat16)
    grad_queries = jnp.einsum(
        "hqk,khd->qhd", grad_scores, keys_bf, preferred_element_type=jnp.float32
    )
    grad_keys = jnp.einsum("hqk,qhd->khd", grad_scores, queries, preferred_element_type=jnp.float32)
    return (grad_queries, grad_keys, grad_values)


CHUNK = 32
BLOCK = 128
NPIECES = 8
LAG = 2
EDGE_LAG = 3
LIMIT = 67043328


def dot(left, right, left_dim, right_dim):
    return lax.dot_general(
        left, right, (((left_dim,), (right_dim,)), ((), ())), preferred_element_type=jnp.float32
    )


def remote(src, dst, send, recv, device):
    return pltpu.make_async_remote_copy(
        src_ref=src,
        dst_ref=dst,
        send_sem=send,
        recv_sem=recv,
        device_id=device,
        device_id_type=MESH,
    )


def push(src, dst, send, recv, device):
    copy = remote(src, dst, send, recv, device)
    copy.start()
    return copy


def greet(peers):
    barrier = pltpu.get_barrier_semaphore()
    for peer in peers:
        pl.semaphore_signal(barrier, inc=1, device_id=peer, device_id_type=MESH)
    pl.semaphore_wait(barrier, len(peers))


class Place:
    def __init__(self):
        dp = self.dp = lax.axis_index("dp")
        me = self.me = lax.axis_index("tensor")
        x = self.x = dp % 2
        line = dp // 2
        y, k = me // 2, me % 2
        self.k = k
        self.inner = (line == 1) | (line == 2)
        self.edge = (line == 0) | (line == 3)
        odd = line % 2
        self.xn = (dp + 1 - 2 * x, me)
        self.yn = (dp, (me + 2) % 4)
        self.cn = (dp, me + 1 - 2 * k)
        self.beside = ((line + 1 - 2 * odd) * 2 + x, me)
        self.mirror = ((3 - line) * 2 + x, me)
        self.q = k * 2 + y
        self.qy = k * 2 + 1 - y
        self.qc = (1 - k) * 2 + y
        self.qcy = (1 - k) * 2 + 1 - y


class Reduce:
    def __init__(self, place, part, rx, mid, ry, send, recv):
        self.p, self.part, self.rx, self.mid, self.ry = place, part, rx, mid, ry
        self.send, self.recv = send, recv

    def start(self):
        p = self.p
        self.c = [
            push(self.part.at[p.qcy], self.rx.at[0], self.send.at[0], self.recv.at[0], p.cn),
            push(self.part.at[p.qc], self.rx.at[1], self.send.at[1], self.recv.at[1], p.cn),
        ]

    def first(self):
        p = self.p
        self.c[0].wait_recv()
        self.mid[...] = self.part[p.qy] + self.rx[0]
        self.c.append(push(self.mid, self.ry, self.send.at[2], self.recv.at[2], p.yn))

    def second(self):
        self.c[1].wait_recv()
        self.rx[1] = self.part[self.p.q] + self.rx[1]

    def wait(self):
        self.c[2].wait_recv()

    def rows(self, at, size):
        return self.rx[1, pl.ds(at, size), :] + self.ry[pl.ds(at, size), :]

    def drain(self):
        for copy in self.c:
            copy.wait_send()


class Gather:
    def __init__(self, place, own, peer, send, recv):
        self.p, self.own, self.peer, self.send, self.recv = place, own, peer, send, recv
        self.c = {}

    def go(self, n, ref, at, device, into=None):
        into = ref if into is None else into
        self.c[n] = push(ref.at[at], into.at[at], self.send.at[n], self.recv.at[n], device)

    def start(self):
        p = self.p
        self.go(0, self.own, p.q, p.yn)
        self.go(3, self.own, p.q, p.cn)
        if self.peer is not None:
            self.go(1, self.own, p.q, p.xn, self.peer)

    def from_y(self):
        self.c[0].wait_recv()
        self.go(4, self.own, self.p.qy, self.p.cn)
        if self.peer is not None:
            self.slip(7, self.own, self.p.qy, 0, self.p.xn)

    def own_done(self):
        self.c[3].wait_recv()
        self.c[4].wait_recv()

    def from_x(self):
        self.c[1].wait_recv()
        self.slip(2, self.peer, self.p.q, 1, self.p.yn)
        self.go(5, self.peer, self.p.q, self.p.cn)

    def slip(self, n, ref, at, part, device):
        size = ref.shape[1] // 2
        rows = pl.ds(part * size, size)
        src, into = ref.at[at, rows], self.peer.at[at, rows]
        self.c[n] = push(src, into, self.send.at[n], self.recv.at[n], device)

    def from_diagonal(self):
        self.c[2].wait_recv()
        self.c[7].wait_recv()
        self.go(6, self.peer, self.p.qy, self.p.cn)

    def peer_done(self):
        self.c[5].wait_recv()
        self.c[6].wait_recv()

    def drain(self):
        for copy in self.c.values():
            copy.wait_send()


class Swap:
    def __init__(self, place, src, dst, send, recv):
        self.p, self.src, self.dst, self.send, self.recv = place, src, dst, send, recv
        half = src.shape[0] // 2
        self.rows = pl.ds(pl.multiple_of(place.k * half, 8), half)

    def start(self):
        src, dst = self.src.at[self.rows], self.dst.at[self.rows]
        self.c = [push(src, dst, self.send.at[0], self.recv.at[0], self.p.xn)]

    def share(self):
        self.c[0].wait_recv()
        dst = self.dst.at[self.rows]
        self.c.append(push(dst, dst, self.send.at[1], self.recv.at[1], self.p.cn))

    def done(self):
        self.c[1].wait_recv()

    def drain(self):
        for copy in self.c:
            copy.wait_send()


def layout(operands):
    rows, width = operands[0].shape
    local, hidden = operands[3].shape[0] // 3, operands[10].shape[1]
    heads, quarter, half = local // HD, rows // 4, hidden // 2
    f32, bf16 = jnp.float32, jnp.bfloat16
    b = types.SimpleNamespace()
    b.args = [pltpu.VMEM(item.shape, item.dtype) for item in operands]
    b.arg_sem = pltpu.SemaphoreType.DMA((len(operands),))

    def mem(*shape, kind=f32):
        return pltpu.VMEM(shape, kind)

    def sems(count):
        return [pltpu.SemaphoreType.DMA((count,))] * 2

    b.tok_f, b.cot_f = mem(rows, width), mem(rows, width)
    b.tok_peer, b.cot_peer = [mem(rows, width)] * 2
    b.swaps = [sems(2)] * 2
    b.len_own, b.len_peer, b.len_sem = mem(8, 128), mem(8, 128), sems(1)
    b.hid1, b.h2, b.cots, b.gms = [mem(2 * rows, width, kind=bf16)] * 4
    b.stack = mem(2 * rows, 4 * 256, kind=bf16)
    b.acth, b.gpreh = [mem(2 * rows, half, kind=bf16)] * 2
    b.act, b.gpre = [mem(rows, hidden, kind=bf16)] * 2
    b.pre, b.gact, b.gact_peer = mem(rows, hidden), mem(rows, hidden), mem(rows, half)
    b.probs = mem(heads, rows, rows)
    b.heads = mem(3 * heads, rows, HD, kind=bf16)
    b.gk, b.gv = mem(rows, HD), mem(rows, HD)
    four, two, one = mem(4, quarter, width), mem(2, quarter, width), mem(quarter, width)
    b.sums = [[four, two, one, one, *sems(3)]] * 4
    b.wide = [[four, four, *sems(8)]] * 2
    b.slim = [[four, *sems(7)]] * 2
    b.middle, b.gmid = one, one
    b.parts = [mem(half, width), mem(width, half), mem(2 * local, width)]
    cut = [(x.shape[0] // NPIECES, x.shape[1]) for x in b.parts]
    b.rz = [mem(NPIECES, *shape) for shape in cut]
    b.ry = [mem(NPIECES, *shape) for shape in cut]
    b.tots = [mem(hidden, width), mem(width, hidden), mem(4 * local, width)]
    b.up, b.cross, b.down, b.give = [sems(3 * NPIECES)] * 4
    b.bias, b.mine = mem(8, hidden), mem(8, width)
    b.notes, b.heard, b.note_sem = mem(5, 8, width), mem(5, 8, width), sems(5)
    b.tiles, b.total = [mem(rows, width, kind=bf16)] * 2, mem(8, width)
    b.out = pltpu.SemaphoreType.DMA((7,))
    return vars(b)


def loop(rows, body, init=None, size=CHUNK):
    if init is None:

        def run(i, _):
            body(pl.multiple_of(i * size, size))
            return 0

        lax.fori_loop(0, rows // size, run, 0)
        return None
    return lax.fori_loop(0, rows // size, lambda i, c: body(pl.multiple_of(i * size, size), c), init)


def column_sum(values):
    return jnp.sum(values, axis=0, keepdims=True)


def block_kernel(tree, *refs):
    (block_out, input_grad, grad_in, grad_out, grad_hidden, grad_down) = refs[16:22]
    small_out = refs[22]
    s = types.SimpleNamespace(**jax.tree.unflatten(tree, refs[23:]))
    (tokens, cot, seg, attn_rows, query_bias, value_bias, attn_output, output_bias) = s.args[:8]
    (gain_one, shift_one, hidden_w, hidden_bias, down_w, down_bias, gain_two, shift_two) = s.args[8:]
    loads = [pltpu.make_async_copy(refs[n], s.args[n], s.arg_sem.at[n]) for n in range(16)]
    for n in (2, 1, 0, 8, 9, 3, 4, 5, 6, 7, 14, 15, 12, 10, 11, 13):
        loads[n].start()

    def ready(*which):
        for n in which:
            loads[n].wait()
    f32, bf16 = jnp.float32, jnp.bfloat16
    rows, width = tokens.shape
    local = attn_rows.shape[0] // 3
    hidden = hidden_w.shape[1]
    heads, quarter, half = local // HD, rows // 4, hidden // 2
    p = Place()

    def line(ref):
        return ref[...].reshape(1, ref.shape[0])

    sum1, sum2, sum3, sum4 = (Reduce(p, *item) for item in s.sums)
    all1, all2 = (Gather(p, *item) for item in s.wide)
    all3, all4 = (Gather(p, own, None, *rest) for own, *rest in s.slim)
    swap_cot = Swap(p, s.cot_f, s.cot_peer, *s.swaps[0])
    swap_tok = Swap(p, s.tok_f, s.tok_peer, *s.swaps[1])

    parts, rz, ry, tots = s.parts, s.rz, s.ry, s.tots
    units = [(m, i) for m in range(3) for i in range(NPIECES)]
    count = len(units)

    def piece(u):
        m, i = units[u]
        size = parts[m].shape[0] // NPIECES
        return parts[m].at[pl.ds(i * size, size)]

    def place_of(u, column):
        m, i = units[u]
        tall, wide = parts[m].shape
        size = tall // NPIECES
        if m == 1:
            return tots[m].at[pl.ds(i * size, size), pl.ds(pl.multiple_of(column * wide, 128), wide)]
        return tots[m].at[pl.ds(pl.multiple_of(column * tall + i * size, 8), size)]

    def hop(sem, src, dst, u, device):
        return remote(src, dst, sem[0].at[u], sem[1].at[u], device)

    def up(u):
        m, i = units[u]
        return hop(s.up, piece(u), rz[m].at[i], u, p.beside)

    def cross(u):
        m, i = units[u]
        return hop(s.cross, piece(u), ry[m].at[i], u, p.mirror)

    def down(u):
        return hop(s.down, place_of(u, p.x), place_of(u, p.x), u, p.beside)

    def give(u):
        return hop(s.give, place_of(u, p.x), place_of(u, p.x), u, p.xn)

    def send_up(us):
        @pl.when(p.edge)
        def _():
            for u in us:
                up(u).start()

    def step(at):
        @pl.when(p.inner)
        def _():
            if at < count:
                m, i = units[at]
                up(at).wait_recv()
                src = piece(at)
                src[...] = src[...] + rz[m][i]
                cross(at).start()
            if 0 <= at - LAG < count:
                u = at - LAG
                m, i = units[u]
                cross(u).wait_recv()
                place_of(u, p.x)[...] = piece(u)[...] + ry[m][i]
                down(u).start()
                give(u).start()

        if 0 <= at - EDGE_LAG < count:

            @pl.when(p.edge)
            def _():
                down(at - EDGE_LAG).wait_recv()
                give(at - EDGE_LAG).start()

    at, sent = [0], [0]

    def pump(n=1):
        for _ in range(n):
            if at[0] < sent[0] or sent[0] == count:
                step(at[0])
                at[0] += 1

    greet([p.xn, p.yn, p.cn, p.beside, p.mirror])
    copies = []

    def emit(src, ref):
        copies.append(pltpu.make_async_copy(src, ref, s.out.at[len(copies)]))
        copies[-1].start()

    ready(1, 2)
    inside = jnp.where(line(seg) >= 0, 1.0, 0.0)
    length = jnp.sum(inside, axis=1, keepdims=True)
    s.len_own[...] = jnp.broadcast_to(length, (8, 128))
    note = push(s.len_own, s.len_peer, s.len_sem[0].at[0], s.len_sem[1].at[0], p.xn)

    def row_index(at, size):
        return (lax.broadcasted_iota(jnp.int32, (size, 1), 0) + at).astype(f32)

    def masked(at):
        keep = row_index(at, CHUNK) < length
        return jnp.where(keep, cot[pl.ds(at, CHUNK), :].astype(f32), 0.0)

    def mask_half(at):
        at = pl.multiple_of(p.k * (rows // 2) + at, CHUNK)
        s.cot_f[pl.ds(at, CHUNK), :] = masked(at)

    def mask_cot(at, total):
        values = masked(at)
        s.cots[pl.ds(at, CHUNK), :] = values.astype(bf16)
        return total + column_sum(values)

    loop(rows // 2, mask_half)
    swap_cot.start()
    ready(0, 8, 9)
    gain1, shift1 = line(gain_one), line(shift_one)

    def first_norm(at):
        t = tokens[pl.ds(at, CHUNK), :].astype(f32)
        s.tok_f[pl.ds(at, CHUNK), :] = t
        s.hid1[pl.ds(at, CHUNK), :] = norm_forward(t, gain1, shift1)[2].astype(bf16)

    loop(rows, first_norm)

    def project(base):
        normal = s.hid1[base : base + rows, :]
        for m in range(3):
            out = dot(normal, attn_rows[m * local : (m + 1) * local, :], 1, 1)
            if m == 0:
                out = (out + line(query_bias)).astype(bf16) * jnp.asarray(HD ** (-0.5), bf16)
            elif m == 1:
                out = out.astype(bf16)
            else:
                out = (out + line(value_bias)).astype(bf16)
            for h in range(heads):
                s.heads[m * heads + h] = out[:, h * HD : (h + 1) * HD]

    def probabilities(h, i, bound):
        top_row, n = i * BLOCK, (i + 1) * BLOCK
        query = s.heads[h, top_row:n, :]
        key = s.heads[heads + h, 0:n, :]
        row = (lax.broadcasted_iota(jnp.int32, (BLOCK, n), 0) + top_row).astype(f32)
        col = lax.broadcasted_iota(jnp.int32, (BLOCK, n), 1).astype(f32)
        allowed = (col <= row) & ((col >= bound) | (row < bound))
        scores = jnp.where(allowed, dot(query, key, 1, 1), -jnp.inf)
        e = jnp.exp(scores - jnp.max(scores, axis=1, keepdims=True))
        return e * (1.0 / jnp.sum(e, axis=1, keepdims=True))

    def mix(h, i, base, probs_bf):
        n = (i + 1) * BLOCK
        value = s.heads[2 * heads + h, 0:n, :]
        mixed = dot(probs_bf, value, 1, 0).astype(bf16)
        at = 3 * 256 + h * HD
        s.stack[base + i * BLOCK : base + n, at : at + HD] = mixed

    def head_back(h, base, get, beats):
        blocks = rows // BLOCK
        for i in reversed(range(blocks)):
            if i in beats:
                pump()
            top_row, n = i * BLOCK, (i + 1) * BLOCK
            r = slice(base + top_row, base + n)
            probs = get(i)
            probs_bf = probs.astype(bf16)
            if base:
                mix(h, i, base, probs_bf)
            mixed = dot(s.gms[r, :], attn_output[h * HD : (h + 1) * HD, :], 1, 1).astype(bf16)
            value = s.heads[2 * heads + h, 0:n, :]
            key = s.heads[heads + h, 0:n, :]
            grad_probs = dot(mixed, value, 1, 1)
            weighted = jnp.sum(probs * grad_probs, axis=1, keepdims=True)
            scores = (probs * (grad_probs - weighted)).astype(bf16)
            query = s.heads[h, top_row:n, :]
            grad_query = dot(scores, key, 1, 0) * HD ** (-0.5)
            grad_key = dot(scores, query, 0, 0)
            grad_value = dot(probs_bf, mixed, 0, 0)
            s.stack[r, h * HD : (h + 1) * HD] = grad_query.astype(bf16)
            if i == blocks - 1:
                query_sum = column_sum(grad_query)
                s.gk[...] = grad_key
                s.gv[...] = grad_value
            else:
                query_sum = query_sum + column_sum(grad_query)
                s.gk[0:n, :] += grad_key
                s.gv[0:n, :] += grad_value
        s.stack[base : base + rows, 256 + h * HD : 256 + (h + 1) * HD] = s.gk[...].astype(bf16)
        s.stack[base : base + rows, 512 + h * HD : 512 + (h + 1) * HD] = s.gv[...].astype(bf16)
        if not base:
            s.mine[2:3, h * HD : (h + 1) * HD] = query_sum
            s.mine[2:3, 256 + h * HD : 256 + (h + 1) * HD] = column_sum(s.gv[...])

    ready(3, 4, 5)
    project(0)
    ready(6)
    for h in range(heads):
        for i in range(rows // BLOCK):
            n = (i + 1) * BLOCK
            probs = probabilities(h, i, length)
            s.probs[h, i * BLOCK : n, 0:n] = probs
            mix(h, i, 0, probs.astype(bf16))
    attended = s.stack[0:rows, 3 * 256 : 3 * 256 + local]
    s.sums[0][0][...] = dot(attended, attn_output[...], 1, 0).reshape(4, quarter, width)
    sum1.start()
    sum1.first()
    sum1.second()
    s.mine[...] = jnp.zeros_like(s.mine)
    s.mine[1:2, :] = loop(rows, mask_cot, jnp.zeros((1, width), f32))
    ready(7, 14, 15, 12)
    gain2, shift2 = line(gain_two), line(shift_two)
    s.gact[...] = dot(s.cots[0:rows, :], down_w[...], 1, 1)

    own_rows = p.q * quarter
    out_bias = line(output_bias)
    sum1.wait()

    def second_norm(at):
        r = pl.ds(pl.multiple_of(own_rows + at, CHUNK), CHUNK)
        middle = s.tok_f[r, :] + sum1.rows(at, CHUNK) + out_bias
        s.middle[pl.ds(at, CHUNK), :] = middle
        normal = norm_forward(middle, gain2, shift2)[2].astype(bf16)
        s.wide[0][0][p.q, pl.ds(at, CHUNK), :] = normal.astype(f32)

    loop(quarter, second_norm)
    all1.start()
    ready(10, 11, 13)
    cut = pl.ds(pl.multiple_of(p.x * half, 128), half)
    swap_cot.share()
    swap_cot.done()
    s.cots[rows:, :] = s.cot_peer[...].astype(bf16)
    s.gact_peer[...] = dot(s.cots[rows:, :], down_w[cut, :], 1, 1)
    all1.from_y()
    all1.from_x()
    swap_tok.start()
    all1.own_done()

    s.h2[0:rows, :] = s.wide[0][0][...].reshape(rows, width).astype(bf16)
    s.pre[...] = dot(s.h2[0:rows, :], hidden_w[...], 1, 0)
    bias = line(hidden_bias)

    def activate(at, total):
        r = pl.ds(at, CHUNK)
        value, slope = gelu_pair(s.pre[r, :] + bias)
        s.act[r, :] = value.astype(bf16)
        grad = s.gact[r, :] * slope
        s.gpre[r, :] = grad.astype(bf16)
        return total + column_sum(grad)

    s.mine[0:1, :] = loop(rows, activate, jnp.zeros((1, hidden), f32))
    s.sums[1][0][...] = dot(s.gpre[...], hidden_w[...], 1, 1).reshape(4, quarter, width)
    sum2.start()
    sum2.first()
    sum2.second()
    s.acth[0:rows, :] = s.act[:, cut]
    s.gpreh[0:rows, :] = s.gpre[:, cut]

    all1.from_diagonal()
    all1.peer_done()
    s.h2[rows:, :] = s.wide[0][1][...].reshape(rows, width).astype(bf16)
    s.pre[:, 0:half] = dot(s.h2[rows:, :], hidden_w[:, cut], 1, 0)
    s.bias[0:1, :] = bias
    bias_half = s.bias[0:1, cut]

    def activate_peer(at):
        r = pl.ds(at, CHUNK)
        low = pl.ds(pl.multiple_of(rows + at, CHUNK), CHUNK)
        value, slope = gelu_pair(s.pre[r, 0:half] + bias_half)
        s.acth[low, :] = value.astype(bf16)
        s.gpreh[low, :] = (s.gact_peer[r, :] * slope).astype(bf16)

    loop(rows, activate_peer)
    parts[0][...] = dot(s.acth[...], s.cots[...], 0, 0)
    send_up(range(NPIECES))
    sent[0] = NPIECES
    parts[1][...] = dot(s.h2[...], s.gpreh[...], 0, 0)
    send_up(range(NPIECES, 2 * NPIECES))
    sent[0] = 2 * NPIECES

    sum2.wait()

    def second_back(at, total):
        r = pl.ds(pl.multiple_of(own_rows + at, CHUNK), CHUNK)
        grad = sum2.rows(at, CHUNK)
        normed, inverse, _ = norm_forward(s.middle[pl.ds(at, CHUNK), :], gain2, shift2)
        mid = s.cot_f[r, :] + norm_backward(grad, normed, inverse, gain2)
        s.gmid[pl.ds(at, CHUNK), :] = mid
        s.wide[1][0][p.q, pl.ds(at, CHUNK), :] = mid.astype(bf16).astype(f32)
        terms = (grad * normed, grad, mid)
        return tuple(t + column_sum(v) for t, v in zip(total, terms))

    sums = loop(quarter, second_back, (jnp.zeros((1, width), f32),) * 3)
    for n, value in enumerate(sums):
        s.mine[3 + n : 4 + n, :] = value
    all2.start()
    s.sums[2][0][...] = dot(s.act[...], down_w[...], 1, 0).reshape(4, quarter, width)
    sum3.start()
    pump(3)
    all2.from_y()
    all2.from_x()
    all2.own_done()
    pump()
    s.gms[0:rows, :] = s.wide[1][0][...].reshape(rows, width).astype(bf16)
    sum3.first()
    sum3.second()
    for h in range(heads):
        get = lambda i: s.probs[h, i * BLOCK : (i + 1) * BLOCK, 0 : (i + 1) * BLOCK]
        head_back(h, 0, get, (1,))
    pump()
    one = dot(s.stack[0:rows, 0:local], attn_rows[0:local, :], 1, 0)
    for m in range(1, 3):
        item = s.stack[0:rows, m * 256 : m * 256 + local]
        one = one + dot(item, attn_rows[m * local : (m + 1) * local, :], 1, 0)
    s.sums[3][0][...] = one.reshape(4, quarter, width)
    sum4.start()
    pump()
    sum4.first()
    sum4.second()
    swap_tok.share()
    all2.from_diagonal()
    swap_tok.done()

    def peer_norm(at):
        low = pl.ds(pl.multiple_of(rows + at, CHUNK), CHUNK)
        t = s.tok_peer[pl.ds(at, CHUNK), :]
        s.hid1[low, :] = norm_forward(t, gain1, shift1)[2].astype(bf16)

    loop(rows, peer_norm)
    project(rows)
    pump()
    all2.peer_done()
    s.gms[rows:, :] = s.wide[1][1][...].reshape(rows, width).astype(bf16)
    note.wait_recv()
    length_peer = s.len_peer[0:1, 0:1]
    for h in range(heads):
        head_back(h, rows, lambda i: probabilities(h, i, length_peer), (1,))
    pump()

    left = s.stack[:, pl.ds(pl.multiple_of(p.x * 512, 128), local)]
    parts[2][0:local, :] = dot(left, s.hid1[...], 0, 0)

    @pl.when(p.x == 0)
    def _():
        parts[2][local:, :] = dot(s.stack[:, 256 : 256 + local], s.hid1[...], 0, 0)

    @pl.when(p.x == 1)
    def _():
        parts[2][local:, :] = dot(s.stack[:, 768 : 768 + local], s.gms[...], 0, 0)

    send_up(range(2 * NPIECES, count))
    sent[0] = count
    pump()
    sum4.wait()

    def first_back(row, total):
        r = pl.ds(pl.multiple_of(own_rows + row, CHUNK), CHUNK)
        grad = sum4.rows(row, CHUNK)
        normed, inverse, _ = norm_forward(s.tok_f[r, :], gain1, shift1)
        back = norm_backward(grad, normed, inverse, gain1)
        s.slim[1][0][p.q, pl.ds(row, CHUNK), :] = s.gmid[pl.ds(row, CHUNK), :] + back
        return tuple(t + column_sum(v) for t, v in zip(total, (grad * normed, grad)))

    sums = loop(quarter, first_back, (jnp.zeros((1, width), f32),) * 2)
    for n, value in enumerate(sums):
        s.mine[6 + n : 7 + n, :] = value
    all4.start()
    notes = []

    def note_out(value, device):
        n = len(notes)
        s.notes[n] = value
        notes.append(push(s.notes.at[n], s.heard.at[n], s.note_sem[0].at[n], s.note_sem[1].at[n], device))

    def note_in():
        notes[-1].wait_recv()
        return s.notes[len(notes) - 1] + s.heard[len(notes) - 1]

    note_out(s.mine[...], p.cn)
    pump()
    sum3.wait()
    bias = line(down_bias)

    def finish_block(row):
        full = s.middle[pl.ds(row, CHUNK), :] + sum3.rows(row, CHUNK) + bias
        valid = row_index(own_rows + row, CHUNK) < length
        s.slim[0][0][p.q, pl.ds(row, CHUNK), :] = jnp.where(valid, full, 0.0)

    loop(quarter, finish_block)
    all3.start()
    pump()
    note_out(note_in(), p.yn)
    pump(2)
    all4.from_y()
    all4.own_done()
    s.tiles[1][...] = s.slim[1][0][...].reshape(rows, width).astype(bf16)
    emit(s.tiles[1], input_grad)
    which = lax.broadcasted_iota(jnp.int32, (8, width), 0)
    note_out(jnp.where(which < 3, s.mine[...], note_in()), p.xn)
    pump(2)
    all3.from_y()
    all3.own_done()
    s.tiles[0][...] = s.slim[0][0][...].reshape(rows, width).astype(bf16)
    emit(s.tiles[0], block_out)
    note_out(note_in(), p.beside)
    pump(2)
    note_out(note_in(), p.mirror)
    pump(3)
    s.total[...] = note_in()
    emit(s.total, small_out)

    def finish(m, targets):
        for u in range(m * NPIECES, (m + 1) * NPIECES):
            give(u).wait_recv()
        for start, ref in targets:
            emit(tots[m].at[pl.ds(start, ref.shape[0])], ref)

    copied = []
    while at[0] < count + EDGE_LAG:
        if at[0] >= count - 2 and not copied:
            finish(0, [(0, grad_down)])
            copied.append(0)
        pump()
    if not copied:
        finish(0, [(0, grad_down)])
    finish(1, [(0, grad_hidden)])
    finish(2, [(0, grad_in), (3 * local, grad_out)])
    for job in (sum1, sum2, sum3, sum4, all1, all2, all3, all4, swap_cot, swap_tok):
        job.drain()
    for copy in [note] + notes:
        copy.wait_send()
    for u in range(count):
        give(u).wait_send()

    @pl.when(p.edge)
    def _():
        for u in range(count):
            up(u).wait_send()

    @pl.when(p.inner)
    def _():
        for u in range(count):
            cross(u).wait_send()
            down(u).wait_send()

    for copy in copies:
        copy.wait()


def emit_kernel(*refs):
    big, small, outs, vecs = refs[:6], refs[6], refs[7:13], refs[13:22]
    held, sem_in, sem_out = refs[22:28], refs[28], refs[29]
    order = (5, 4, 2, 3, 0, 1)
    reads = {n: pltpu.make_async_copy(big[n], held[n], sem_in.at[n]) for n in order}
    writes = {n: pltpu.make_async_copy(held[n], outs[n], sem_out.at[n]) for n in order}
    for n in order:
        reads[n].start()
    places = [(2, 0), (2, 256), (5, 0), (6, 0), (7, 0), (0, 0), (1, 0), (3, 0), (4, 0)]
    for ref, (row, lane) in zip(vecs, places):
        size = ref.shape[0]
        ref[...] = small[row : row + 1, lane : lane + size].reshape(size)
    for n in order:
        reads[n].wait()
        writes[n].start()
    for n in order:
        writes[n].wait()


def whole_block(operands):
    rows, width = operands[0].shape
    local = operands[3].shape[0] // 3
    hidden = operands[10].shape[1]
    f32 = jnp.float32
    scratch, tree = jax.tree.flatten(layout(operands))
    tile = jax.ShapeDtypeStruct((rows, width), jnp.bfloat16)
    mats = [(3 * local, width), (local, width), (width, hidden), (hidden, width)]
    vecs = [local, local, width, width, width, hidden, width, width, width]
    big = [tile, tile] + [jax.ShapeDtypeStruct(shape, f32) for shape in mats]
    anywhere = pl.BlockSpec(memory_space=pl.ANY)
    results = pl.pallas_call(
        lambda *refs: block_kernel(tree, *refs),
        out_shape=big + [jax.ShapeDtypeStruct((8, width), f32)],
        in_specs=[anywhere] * len(operands),
        out_specs=[anywhere] * 7,
        scratch_shapes=scratch,
        compiler_params=pltpu.CompilerParams(
            collective_id=0, has_side_effects=True, vmem_limit_bytes=LIMIT
        ),
        name="whole_block",
    )(*operands)
    return pl.pallas_call(
        emit_kernel,
        out_shape=big + [jax.ShapeDtypeStruct((n,), f32) for n in vecs],
        in_specs=[anywhere] * 6 + [VM],
        out_specs=[anywhere] * 6 + [VM] * 9,
        scratch_shapes=[pltpu.VMEM(item.shape, item.dtype) for item in big]
        + [pltpu.SemaphoreType.DMA((6,))] * 2,
        compiler_params=pltpu.CompilerParams(vmem_limit_bytes=LIMIT),
        name="emit",
    )(*results)


def plain_shards(
    tokens,
    segment_ids,
    cotangent,
    attn_input,
    query_bias,
    value_bias,
    attn_output,
    output_bias,
    gain_first,
    shift_first,
    hidden_weight,
    hidden_bias,
    down_weight,
    down_bias,
    gain_second,
    shift_second,
):
    row_count = tokens.shape[0]
    local_width = attn_input.shape[2]
    valid = (segment_ids >= 0)[:, None]
    cot_masked = jnp.where(valid, cotangent, jnp.zeros_like(cotangent))
    allowed = allowed_mask(segment_ids)
    resid_in = tokens.astype(jnp.float32)
    normed_one, inverse_one, pre_one = norm_forward(resid_in, gain_first, shift_first)
    hidden_one = pre_one.astype(jnp.bfloat16)
    projected = jnp.einsum(
        "rd,tdc->trc", hidden_one, attn_input, preferred_element_type=jnp.float32
    )
    queries = (projected[0] + query_bias).astype(jnp.bfloat16).reshape(row_count, -1, HD)
    keys_bf = projected[1].astype(jnp.bfloat16).reshape(row_count, -1, HD)
    values_bf = (projected[2] + value_bias).astype(jnp.bfloat16).reshape(row_count, -1, HD)
    mixed, log_sum = attend(queries, keys_bf, values_bf, allowed)
    attended = mixed.reshape(row_count, local_width).astype(jnp.bfloat16)
    attn_part = jnp.dot(attended, attn_output, preferred_element_type=jnp.float32)
    middle = resid_in + lax.psum(attn_part, "tensor") + output_bias
    normed_two, inverse_two, pre_two = norm_forward(middle, gain_second, shift_second)
    hidden_two = pre_two.astype(jnp.bfloat16)
    pre_act = jnp.dot(hidden_two, hidden_weight, preferred_element_type=jnp.float32) + hidden_bias
    gelu_value, gelu_slope = gelu_pair(pre_act)
    activation = gelu_value.astype(jnp.bfloat16)
    mlp_part = jnp.dot(activation, down_weight, preferred_element_type=jnp.float32)
    out_full = middle + lax.psum(mlp_part, "tensor") + down_bias
    block_out = jnp.where(valid, out_full, jnp.zeros_like(out_full)).astype(jnp.bfloat16)
    grad_top = cot_masked.astype(jnp.float32)
    grad_down_bias = jnp.sum(grad_top, axis=0)
    grad_down_weight = contract_rows(activation, cot_masked)
    grad_pre = contract_cols(cot_masked, down_weight) * gelu_slope
    grad_hidden_bias = jnp.sum(grad_pre, axis=0)
    grad_pre_bf = grad_pre.astype(jnp.bfloat16)
    grad_hidden_weight = contract_rows(hidden_two, grad_pre_bf)
    grad_two = lax.psum(contract_cols(grad_pre_bf, hidden_weight), "tensor")
    grad_gain_second = jnp.sum(grad_two * normed_two, axis=0)
    grad_shift_second = jnp.sum(grad_two, axis=0)
    grad_middle = grad_top + norm_backward(grad_two, normed_two, inverse_two, gain_second)
    grad_output_bias = jnp.sum(grad_middle, axis=0)
    grad_middle_bf = grad_middle.astype(jnp.bfloat16)
    grad_attn_output = contract_rows(attended, grad_middle_bf)
    grad_attended = (
        contract_cols(grad_middle_bf, attn_output).astype(jnp.bfloat16).reshape(row_count, -1, HD)
    )
    grad_queries, grad_keys, grad_values = attend_back(
        queries, keys_bf, values_bf, allowed, log_sum, grad_attended
    )
    grad_queries = grad_queries.reshape(row_count, local_width)
    grad_keys = grad_keys.reshape(row_count, local_width)
    grad_values = grad_values.reshape(row_count, local_width)
    grad_query_bias = jnp.sum(grad_queries, axis=0)
    grad_value_bias = jnp.sum(grad_values, axis=0)
    grad_stack = jnp.stack([grad_queries, grad_keys, grad_values]).astype(jnp.bfloat16)
    grad_attn_input = jnp.einsum(
        "rd,trc->tdc", hidden_one, grad_stack, preferred_element_type=jnp.float32
    )
    one_part = jnp.einsum("trc,tdc->rd", grad_stack, attn_input, preferred_element_type=jnp.float32)
    grad_one = lax.psum(one_part, "tensor")
    grad_gain_first = jnp.sum(grad_one * normed_one, axis=0)
    grad_shift_first = jnp.sum(grad_one, axis=0)
    input_grad = (
        grad_middle + norm_backward(grad_one, normed_one, inverse_one, gain_first)
    ).astype(jnp.bfloat16)
    (
        grad_attn_input,
        grad_query_bias,
        grad_value_bias,
        grad_attn_output,
        grad_output_bias,
        grad_gain_first,
        grad_shift_first,
        grad_hidden_weight,
        grad_hidden_bias,
        grad_down_weight,
        grad_down_bias,
        grad_gain_second,
        grad_shift_second,
    ) = lax.psum(
        (
            grad_attn_input,
            grad_query_bias,
            grad_value_bias,
            grad_attn_output,
            grad_output_bias,
            grad_gain_first,
            grad_shift_first,
            grad_hidden_weight,
            grad_hidden_bias,
            grad_down_weight,
            grad_down_bias,
            grad_gain_second,
            grad_shift_second,
        ),
        "dp",
    )
    return (
        block_out,
        input_grad,
        grad_attn_input,
        grad_query_bias,
        grad_value_bias,
        grad_attn_output,
        grad_output_bias,
        grad_gain_first,
        grad_shift_first,
        grad_hidden_weight,
        grad_hidden_bias,
        grad_down_weight,
        grad_down_bias,
        grad_gain_second,
        grad_shift_second,
    )


def shards(
    tokens,
    segment_ids,
    cotangent,
    attn_input,
    query_bias,
    value_bias,
    attn_output,
    output_bias,
    gain_first,
    shift_first,
    hidden_weight,
    hidden_bias,
    down_weight,
    down_bias,
    gain_second,
    shift_second,
):
    if lax.axis_size("tensor") != 4 or lax.axis_size("dp") != 8:
        return plain_shards(
            tokens,
            segment_ids,
            cotangent,
            attn_input,
            query_bias,
            value_bias,
            attn_output,
            output_bias,
            gain_first,
            shift_first,
            hidden_weight,
            hidden_bias,
            down_weight,
            down_bias,
            gain_second,
            shift_second,
        )
    local_width = attn_input.shape[2]
    width = tokens.shape[1]
    operands = (
        tokens,
        cotangent,
        segment_ids,
        attn_input.transpose(0, 2, 1).reshape(3 * local_width, width),
        query_bias,
        value_bias,
        attn_output,
        output_bias,
        gain_first,
        shift_first,
        hidden_weight,
        hidden_bias,
        down_weight,
        down_bias,
        gain_second,
        shift_second,
    )
    (
        block_out,
        input_grad,
        grad_in,
        grad_attn_output,
        grad_hidden_weight,
        grad_down_weight,
        grad_query_bias,
        grad_value_bias,
        grad_output_bias,
        grad_gain_first,
        grad_shift_first,
        grad_hidden_bias,
        grad_down_bias,
        grad_gain_second,
        grad_shift_second,
    ) = whole_block(operands)
    return (
        block_out,
        input_grad,
        grad_in.reshape(3, local_width, width).transpose(0, 2, 1),
        grad_query_bias,
        grad_value_bias,
        grad_attn_output,
        grad_output_bias,
        grad_gain_first,
        grad_shift_first,
        grad_hidden_weight,
        grad_hidden_bias,
        grad_down_weight,
        grad_down_bias,
        grad_gain_second,
        grad_shift_second,
    )


def solution(mesh):
    return jax.shard_map(
        shards,
        mesh=mesh,
        in_specs=(
            P("dp", None),
            P("dp"),
            P("dp", None),
            P(None, None, "tensor"),
            P("tensor"),
            P("tensor"),
            P("tensor", None),
            P(),
            P(),
            P(),
            P(None, "tensor"),
            P("tensor"),
            P("tensor", None),
            P(),
            P(),
            P(),
        ),
        out_specs=(
            P("dp", None),
            P("dp", None),
            P(None, None, "tensor"),
            P("tensor"),
            P("tensor"),
            P("tensor", None),
            P(),
            P(),
            P(),
            P(None, "tensor"),
            P("tensor"),
            P("tensor", None),
            P(),
            P(),
            P(),
        ),
        check_vma=False,
    )
```

```python
import types

import jax
import jax.numpy as jnp
from jax import lax
from jax.experimental import pallas as pl
from jax.experimental.pallas import tpu as pltpu
from jax.sharding import PartitionSpec as P

HD = 64
MESH = pl.DeviceIdType.MESH
VM = pl.BlockSpec(memory_space=pltpu.VMEM)


EPSILON = 1e-05
TANH_SCALE = 0.7978845608028654
CUBIC = 0.044715


def norm_forward(values_in, norm_gain, norm_shift):
    row_mean = jnp.mean(values_in, axis=-1, keepdims=True)
    centered = values_in - row_mean
    inverse = lax.rsqrt(jnp.mean(centered * centered, axis=-1, keepdims=True) + EPSILON)
    normed = centered * inverse
    return (normed, inverse, normed * norm_gain + norm_shift)


def norm_backward(grad_out, normed, inverse, norm_gain):
    scaled = grad_out * norm_gain
    return inverse * (
        scaled
        - jnp.mean(scaled, axis=-1, keepdims=True)
        - normed * jnp.mean(scaled * normed, axis=-1, keepdims=True)
    )


def gelu_pair(pre_act):
    tangent = jnp.tanh(TANH_SCALE * (pre_act + CUBIC * pre_act * pre_act * pre_act))
    gelu_value = 0.5 * pre_act * (1.0 + tangent)
    gelu_slope = 0.5 * (1.0 + tangent) + 0.5 * pre_act * (1.0 - tangent * tangent) * TANH_SCALE * (
        1.0 + 3.0 * CUBIC * pre_act * pre_act
    )
    return (gelu_value, gelu_slope)


def contract_rows(left_mat, right_mat):
    return lax.dot_general(
        left_mat, right_mat, (((0,), (0,)), ((), ())), preferred_element_type=jnp.float32
    )


def contract_cols(left_mat, right_mat):
    return lax.dot_general(
        left_mat, right_mat, (((1,), (1,)), ((), ())), preferred_element_type=jnp.float32
    )


def allowed_mask(segments):
    position = jnp.arange(segments.shape[0])
    return (segments[:, None] == segments[None, :]) & (position[None, :] <= position[:, None])


def head_scores(queries, keys_bf, allowed):
    scaling = queries.shape[-1] ** (-0.5)
    scores = (
        jnp.einsum("qhd,khd->hqk", queries, keys_bf, preferred_element_type=jnp.float32) * scaling
    )
    return jnp.where(allowed[None], scores, -jnp.inf)


def attend(queries, keys_bf, values_bf, allowed):
    scores = head_scores(queries, keys_bf, allowed)
    top_score = jnp.max(scores, axis=-1, keepdims=True)
    log_sum = top_score + jnp.log(jnp.sum(jnp.exp(scores - top_score), axis=-1, keepdims=True))
    probs = jnp.exp(scores - log_sum).astype(jnp.bfloat16)
    mixed = jnp.einsum("hqk,khd->qhd", probs, values_bf, preferred_element_type=jnp.float32)
    return (mixed, log_sum)


def attend_back(queries, keys_bf, values_bf, allowed, log_sum, grad_mixed):
    probs_full = jnp.exp(head_scores(queries, keys_bf, allowed) - log_sum)
    probs_bf = probs_full.astype(jnp.bfloat16)
    grad_values = jnp.einsum(
        "hqk,qhd->khd", probs_bf, grad_mixed, preferred_element_type=jnp.float32
    )
    grad_probs = jnp.einsum(
        "qhd,khd->hqk", grad_mixed, values_bf, preferred_element_type=jnp.float32
    )
    scaling = queries.shape[-1] ** (-0.5)
    grad_scores = (
        probs_full
        * (grad_probs - jnp.sum(probs_full * grad_probs, axis=-1, keepdims=True))
        * scaling
    ).astype(jnp.bfloat16)
    grad_queries = jnp.einsum(
        "hqk,khd->qhd", grad_scores, keys_bf, preferred_element_type=jnp.float32
    )
    grad_keys = jnp.einsum("hqk,qhd->khd", grad_scores, queries, preferred_element_type=jnp.float32)
    return (grad_queries, grad_keys, grad_values)


CHUNK = 32
BLOCK = 128
NPIECES = 8
LAG = 2
EDGE_LAG = 3
LIMIT = 55 * 1024 * 1024


def dot(left, right, left_dim, right_dim):
    return lax.dot_general(
        left, right, (((left_dim,), (right_dim,)), ((), ())), preferred_element_type=jnp.float32
    )


def remote(src, dst, send, recv, device):
    return pltpu.make_async_remote_copy(
        src_ref=src,
        dst_ref=dst,
        send_sem=send,
        recv_sem=recv,
        device_id=device,
        device_id_type=MESH,
    )


def push(src, dst, send, recv, device):
    copy = remote(src, dst, send, recv, device)
    copy.start()
    return copy


def greet(peers):
    barrier = pltpu.get_barrier_semaphore()
    for peer in peers:
        pl.semaphore_signal(barrier, inc=1, device_id=peer, device_id_type=MESH)
    pl.semaphore_wait(barrier, len(peers))


class Place:
    def __init__(self):
        dp = self.dp = lax.axis_index("dp")
        me = self.me = lax.axis_index("tensor")
        x = self.x = dp % 2
        line = dp // 2
        y, k = me // 2, me % 2
        self.k = k
        self.inner = (line == 1) | (line == 2)
        self.edge = (line == 0) | (line == 3)
        odd = line % 2
        self.xn = (dp + 1 - 2 * x, me)
        self.yn = (dp, (me + 2) % 4)
        self.cn = (dp, me + 1 - 2 * k)
        self.beside = ((line + 1 - 2 * odd) * 2 + x, me)
        self.mirror = ((3 - line) * 2 + x, me)
        self.q = k * 2 + y
        self.qy = k * 2 + 1 - y
        self.qc = (1 - k) * 2 + y
        self.qcy = (1 - k) * 2 + 1 - y


class Reduce:
    def __init__(self, place, part, rx, mid, ry, send, recv):
        self.p, self.part, self.rx, self.mid, self.ry = place, part, rx, mid, ry
        self.send, self.recv = send, recv

    def start(self):
        p = self.p
        self.c = [
            push(self.part.at[p.qcy], self.rx.at[0], self.send.at[0], self.recv.at[0], p.cn),
            push(self.part.at[p.qc], self.rx.at[1], self.send.at[1], self.recv.at[1], p.cn),
        ]

    def first(self):
        p = self.p
        self.c[0].wait_recv()
        self.mid[...] = self.part[p.qy] + self.rx[0]
        self.c.append(push(self.mid, self.ry, self.send.at[2], self.recv.at[2], p.yn))

    def second(self):
        self.c[1].wait_recv()
        self.rx[1] = self.part[self.p.q] + self.rx[1]

    def wait(self):
        self.c[2].wait_recv()

    def rows(self, at, size):
        return self.rx[1, pl.ds(at, size), :] + self.ry[pl.ds(at, size), :]

    def drain(self):
        for copy in self.c:
            copy.wait_send()


class Gather:
    def __init__(self, place, own, peer, send, recv):
        self.p, self.own, self.peer, self.send, self.recv = place, own, peer, send, recv
        self.c = {}

    def go(self, n, ref, at, device, into=None):
        into = ref if into is None else into
        self.c[n] = push(ref.at[at], into.at[at], self.send.at[n], self.recv.at[n], device)

    def start(self):
        p = self.p
        self.go(0, self.own, p.q, p.yn)
        self.go(3, self.own, p.q, p.cn)
        if self.peer is not None:
            self.go(1, self.own, p.q, p.xn, self.peer)

    def from_y(self):
        self.c[0].wait_recv()
        self.go(4, self.own, self.p.qy, self.p.cn)
        if self.peer is not None:
            self.slip(7, self.own, self.p.qy, 0, self.p.xn)

    def own_done(self):
        self.c[3].wait_recv()
        self.c[4].wait_recv()

    def from_x(self):
        self.c[1].wait_recv()
        self.slip(2, self.peer, self.p.q, 1, self.p.yn)
        self.go(5, self.peer, self.p.q, self.p.cn)

    def slip(self, n, ref, at, part, device):
        size = ref.shape[1] // 2
        rows = pl.ds(part * size, size)
        src, into = ref.at[at, rows], self.peer.at[at, rows]
        self.c[n] = push(src, into, self.send.at[n], self.recv.at[n], device)

    def from_diagonal(self):
        self.c[2].wait_recv()
        self.c[7].wait_recv()
        self.go(6, self.peer, self.p.qy, self.p.cn)

    def peer_done(self):
        self.c[5].wait_recv()
        self.c[6].wait_recv()

    def drain(self):
        for copy in self.c.values():
            copy.wait_send()


class Swap:
    def __init__(self, place, src, dst, send, recv):
        self.p, self.src, self.dst, self.send, self.recv = place, src, dst, send, recv
        half = src.shape[0] // 2
        self.rows = pl.ds(pl.multiple_of(place.k * half, 8), half)

    def start(self):
        src, dst = self.src.at[self.rows], self.dst.at[self.rows]
        self.c = [push(src, dst, self.send.at[0], self.recv.at[0], self.p.xn)]

    def share(self):
        self.c[0].wait_recv()
        dst = self.dst.at[self.rows]
        self.c.append(push(dst, dst, self.send.at[1], self.recv.at[1], self.p.cn))

    def done(self):
        self.c[1].wait_recv()

    def drain(self):
        for copy in self.c:
            copy.wait_send()


def layout(operands):
    rows, width = operands[0].shape
    local, hidden = operands[3].shape[0] // 3, operands[10].shape[1]
    heads, quarter, half = local // HD, rows // 4, hidden // 2
    f32, bf16 = jnp.float32, jnp.bfloat16
    b = types.SimpleNamespace()
    b.args = [pltpu.VMEM(item.shape, item.dtype) for item in operands]
    b.arg_sem = pltpu.SemaphoreType.DMA((len(operands),))

    def mem(*shape, kind=f32):
        return pltpu.VMEM(shape, kind)

    def sems(count):
        return [pltpu.SemaphoreType.DMA((count,))] * 2

    b.tok_f, b.cot_f = mem(rows, width), mem(rows, width)
    b.tok_peer, b.cot_peer = [mem(rows, width)] * 2
    b.swaps = [sems(2)] * 2
    b.len_own, b.len_peer, b.len_sem = mem(8, 128), mem(8, 128), sems(1)
    b.hid1, b.h2, b.cots, b.gms = [mem(2 * rows, width, kind=bf16)] * 4
    b.stack = mem(2 * rows, 4 * 256, kind=bf16)
    b.acth, b.gpreh = [mem(2 * rows, half, kind=bf16)] * 2
    b.act, b.gpre = [mem(rows, hidden, kind=bf16)] * 2
    b.pre, b.gact, b.gact_peer = mem(rows, hidden), mem(rows, hidden), mem(rows, half)
    b.probs = mem(heads, rows, rows)
    b.heads = mem(3 * heads, rows, HD, kind=bf16)
    b.gk, b.gv = mem(rows, HD), mem(rows, HD)
    four, two, one = mem(4, quarter, width), mem(2, quarter, width), mem(quarter, width)
    b.sums = [[four, two, one, one, *sems(3)]] * 4
    b.wide = [[four, four, *sems(8)]] * 2
    b.slim = [[four, *sems(7)]] * 2
    b.middle, b.gmid = one, one
    b.parts = [mem(half, width), mem(width, half), mem(2 * local, width)]
    cut = [(x.shape[0] // NPIECES, x.shape[1]) for x in b.parts]
    b.rz = [mem(NPIECES, *shape) for shape in cut]
    b.ry = [mem(NPIECES, *shape) for shape in cut]
    b.up, b.cross, b.down, b.give = [sems(3 * NPIECES)] * 4
    b.bias, b.mine = mem(8, hidden), mem(8, width)
    b.notes, b.heard, b.note_sem = mem(5, 8, width), mem(5, 8, width), sems(5)
    return vars(b)


def loop(rows, body, init=None, size=CHUNK):
    if init is None:

        def run(i, _):
            body(pl.multiple_of(i * size, size))
            return 0

        lax.fori_loop(0, rows // size, run, 0)
        return None
    return lax.fori_loop(0, rows // size, lambda i, c: body(pl.multiple_of(i * size, size), c), init)


def column_sum(values):
    return jnp.sum(values, axis=0, keepdims=True)


def block_kernel(tree, *refs):
    block_out, input_grad = refs[16:18]
    tots, small_out = refs[18:21], refs[21]
    s = types.SimpleNamespace(**jax.tree.unflatten(tree, refs[22:]))
    (tokens, cot, seg, attn_rows, query_bias, value_bias, attn_output, output_bias) = s.args[:8]
    (gain_one, shift_one, hidden_w, hidden_bias, down_w, down_bias, gain_two, shift_two) = s.args[8:]
    loads = [pltpu.make_async_copy(refs[n], s.args[n], s.arg_sem.at[n]) for n in range(16)]
    for n in (2, 1, 0, 8, 9, 3, 4, 5, 6, 7, 14, 15, 12, 10, 11, 13):
        loads[n].start()

    def ready(*which):
        for n in which:
            loads[n].wait()
    f32, bf16 = jnp.float32, jnp.bfloat16
    rows, width = tokens.shape
    local = attn_rows.shape[0] // 3
    hidden = hidden_w.shape[1]
    heads, quarter, half = local // HD, rows // 4, hidden // 2
    p = Place()

    def line(ref):
        return ref[...].reshape(1, ref.shape[0])

    sum1, sum2, sum3, sum4 = (Reduce(p, *item) for item in s.sums)
    all1, all2 = (Gather(p, *item) for item in s.wide)
    all3, all4 = (Gather(p, own, None, *rest) for own, *rest in s.slim)
    swap_cot = Swap(p, s.cot_f, s.cot_peer, *s.swaps[0])
    swap_tok = Swap(p, s.tok_f, s.tok_peer, *s.swaps[1])

    parts, rz, ry = s.parts, s.rz, s.ry
    units = [(m, i) for m in range(3) for i in range(NPIECES)]
    count = len(units)

    def piece(u):
        m, i = units[u]
        size = parts[m].shape[0] // NPIECES
        return parts[m].at[pl.ds(i * size, size)]

    def place_of(u, column):
        m, i = units[u]
        tall, wide = parts[m].shape
        size = tall // NPIECES
        if m == 1:
            return tots[m].at[pl.ds(i * size, size), pl.ds(pl.multiple_of(column * wide, 128), wide)]
        return tots[m].at[pl.ds(pl.multiple_of(column * tall + i * size, 8), size)]

    def hop(sem, src, dst, u, device):
        return remote(src, dst, sem[0].at[u], sem[1].at[u], device)

    def up(u):
        m, i = units[u]
        return hop(s.up, piece(u), rz[m].at[i], u, p.beside)

    def cross(u):
        m, i = units[u]
        return hop(s.cross, piece(u), ry[m].at[i], u, p.mirror)

    def down(u):
        return hop(s.down, place_of(u, p.x), place_of(u, p.x), u, p.beside)

    def give(u):
        return hop(s.give, place_of(u, p.x), place_of(u, p.x), u, p.xn)

    def send_up(us):
        @pl.when(p.edge)
        def _():
            for u in us:
                up(u).start()

    def step(at):
        @pl.when(p.inner)
        def _():
            if at < count:
                m, i = units[at]
                up(at).wait_recv()
                src = piece(at)
                src[...] = src[...] + rz[m][i]
                cross(at).start()
            if 0 <= at - LAG < count:
                u = at - LAG
                m, i = units[u]
                cross(u).wait_recv()
                place_of(u, p.x)[...] = piece(u)[...] + ry[m][i]
                down(u).start()
                give(u).start()

        if 0 <= at - EDGE_LAG < count:

            @pl.when(p.edge)
            def _():
                down(at - EDGE_LAG).wait_recv()
                give(at - EDGE_LAG).start()

    at, sent = [0], [0]

    def pump(n=1):
        for _ in range(n):
            if at[0] < sent[0] or sent[0] == count:
                step(at[0])
                at[0] += 1

    greet([p.xn, p.yn, p.cn, p.beside, p.mirror])
    ready(1, 2)
    inside = jnp.where(line(seg) >= 0, 1.0, 0.0)
    length = jnp.sum(inside, axis=1, keepdims=True)
    s.len_own[...] = jnp.broadcast_to(length, (8, 128))
    note = push(s.len_own, s.len_peer, s.len_sem[0].at[0], s.len_sem[1].at[0], p.xn)

    def row_index(at, size):
        return (lax.broadcasted_iota(jnp.int32, (size, 1), 0) + at).astype(f32)

    def masked(at):
        keep = row_index(at, CHUNK) < length
        return jnp.where(keep, cot[pl.ds(at, CHUNK), :].astype(f32), 0.0)

    def mask_half(at):
        at = pl.multiple_of(p.k * (rows // 2) + at, CHUNK)
        s.cot_f[pl.ds(at, CHUNK), :] = masked(at)

    def mask_cot(at, total):
        values = masked(at)
        s.cots[pl.ds(at, CHUNK), :] = values.astype(bf16)
        return total + column_sum(values)

    loop(rows // 2, mask_half)
    swap_cot.start()
    ready(0, 8, 9)
    gain1, shift1 = line(gain_one), line(shift_one)

    def first_norm(at):
        t = tokens[pl.ds(at, CHUNK), :].astype(f32)
        s.tok_f[pl.ds(at, CHUNK), :] = t
        s.hid1[pl.ds(at, CHUNK), :] = norm_forward(t, gain1, shift1)[2].astype(bf16)

    loop(rows, first_norm)

    def project(base):
        normal = s.hid1[base : base + rows, :]
        for m in range(3):
            out = dot(normal, attn_rows[m * local : (m + 1) * local, :], 1, 1)
            if m == 0:
                out = (out + line(query_bias)).astype(bf16) * jnp.asarray(HD ** (-0.5), bf16)
            elif m == 1:
                out = out.astype(bf16)
            else:
                out = (out + line(value_bias)).astype(bf16)
            for h in range(heads):
                s.heads[m * heads + h] = out[:, h * HD : (h + 1) * HD]

    def probabilities(h, i, bound):
        top_row, n = i * BLOCK, (i + 1) * BLOCK
        query = s.heads[h, top_row:n, :]
        key = s.heads[heads + h, 0:n, :]
        row = (lax.broadcasted_iota(jnp.int32, (BLOCK, n), 0) + top_row).astype(f32)
        col = lax.broadcasted_iota(jnp.int32, (BLOCK, n), 1).astype(f32)
        allowed = (col <= row) & ((col >= bound) | (row < bound))
        scores = jnp.where(allowed, dot(query, key, 1, 1), -jnp.inf)
        e = jnp.exp(scores - jnp.max(scores, axis=1, keepdims=True))
        return e * (1.0 / jnp.sum(e, axis=1, keepdims=True))

    def mix(h, i, base, probs_bf):
        n = (i + 1) * BLOCK
        value = s.heads[2 * heads + h, 0:n, :]
        mixed = dot(probs_bf, value, 1, 0).astype(bf16)
        at = 3 * 256 + h * HD
        s.stack[base + i * BLOCK : base + n, at : at + HD] = mixed

    def head_back(h, base, get, beats):
        blocks = rows // BLOCK
        sums = []

        def only(x, body):
            if base:
                pl.when(p.x == x)(body)
            else:
                body()

        def into(ref, n, value, first):
            if first:
                ref[...] = value
            else:
                ref[0:n, :] += value

        for i in reversed(range(blocks)):
            if i in beats:
                pump()
            top_row, n = i * BLOCK, (i + 1) * BLOCK
            r = slice(base + top_row, base + n)
            probs = get(i)
            mixed = dot(s.gms[r, :], attn_output[h * HD : (h + 1) * HD, :], 1, 1).astype(bf16)

            def values():
                probs_bf = probs.astype(bf16)
                if base:
                    mix(h, i, base, probs_bf)
                into(s.gv, n, dot(probs_bf, mixed, 0, 0), i == blocks - 1)

            def scores():
                value = s.heads[2 * heads + h, 0:n, :]
                key = s.heads[heads + h, 0:n, :]
                grad_probs = dot(mixed, value, 1, 1)
                weighted = jnp.sum(probs * grad_probs, axis=1, keepdims=True)
                grad = (probs * (grad_probs - weighted)).astype(bf16)
                query = s.heads[h, top_row:n, :]
                grad_query = dot(grad, key, 1, 0) * HD ** (-0.5)
                into(s.gk, n, dot(grad, query, 0, 0), i == blocks - 1)
                s.stack[r, h * HD : (h + 1) * HD] = grad_query.astype(bf16)
                if not base:
                    sums.append(column_sum(grad_query))

            only(0, scores)
            only(1, values)

        def store(at, ref):
            s.stack[base : base + rows, at + h * HD : at + (h + 1) * HD] = ref[...].astype(bf16)

        only(0, lambda: store(256, s.gk))
        only(1, lambda: store(512, s.gv))
        if not base:
            s.mine[2:3, h * HD : (h + 1) * HD] = sum(sums[1:], sums[0])
            s.mine[2:3, 256 + h * HD : 256 + (h + 1) * HD] = column_sum(s.gv[...])

    ready(3, 4, 5)
    project(0)
    ready(6)
    for h in range(heads):
        for i in range(rows // BLOCK):
            n = (i + 1) * BLOCK
            probs = probabilities(h, i, length)
            s.probs[h, i * BLOCK : n, 0:n] = probs
            mix(h, i, 0, probs.astype(bf16))
    attended = s.stack[0:rows, 3 * 256 : 3 * 256 + local]
    s.sums[0][0][...] = dot(attended, attn_output[...], 1, 0).reshape(4, quarter, width)
    sum1.start()
    sum1.first()
    sum1.second()
    s.mine[...] = jnp.zeros_like(s.mine)
    s.mine[1:2, :] = loop(rows, mask_cot, jnp.zeros((1, width), f32))
    ready(7, 14, 15, 12)
    gain2, shift2 = line(gain_two), line(shift_two)
    s.gact[...] = dot(s.cots[0:rows, :], down_w[...], 1, 1)

    own_rows = p.q * quarter
    out_bias = line(output_bias)
    sum1.wait()

    def second_norm(at):
        r = pl.ds(pl.multiple_of(own_rows + at, CHUNK), CHUNK)
        middle = s.tok_f[r, :] + sum1.rows(at, CHUNK) + out_bias
        s.middle[pl.ds(at, CHUNK), :] = middle
        normal = norm_forward(middle, gain2, shift2)[2].astype(bf16)
        s.wide[0][0][p.q, pl.ds(at, CHUNK), :] = normal.astype(f32)

    loop(quarter, second_norm)
    all1.start()
    ready(10, 11, 13)
    cut = pl.ds(pl.multiple_of(p.x * half, 128), half)
    swap_cot.share()
    swap_cot.done()
    s.cots[rows:, :] = s.cot_peer[...].astype(bf16)
    s.gact_peer[...] = dot(s.cots[rows:, :], down_w[cut, :], 1, 1)
    all1.from_y()
    all1.from_x()
    swap_tok.start()
    all1.own_done()

    s.h2[0:rows, :] = s.wide[0][0][...].reshape(rows, width).astype(bf16)
    s.pre[...] = dot(s.h2[0:rows, :], hidden_w[...], 1, 0)
    bias = line(hidden_bias)

    def activate(at, total):
        r = pl.ds(at, CHUNK)
        value, slope = gelu_pair(s.pre[r, :] + bias)
        s.act[r, :] = value.astype(bf16)
        grad = s.gact[r, :] * slope
        s.gpre[r, :] = grad.astype(bf16)
        return total + column_sum(grad)

    s.mine[0:1, :] = loop(rows, activate, jnp.zeros((1, hidden), f32))
    s.sums[1][0][...] = dot(s.gpre[...], hidden_w[...], 1, 1).reshape(4, quarter, width)
    sum2.start()
    sum2.first()
    sum2.second()
    s.acth[0:rows, :] = s.act[:, cut]
    s.gpreh[0:rows, :] = s.gpre[:, cut]

    all1.from_diagonal()
    all1.peer_done()
    s.h2[rows:, :] = s.wide[0][1][...].reshape(rows, width).astype(bf16)
    s.pre[:, 0:half] = dot(s.h2[rows:, :], hidden_w[:, cut], 1, 0)
    s.bias[0:1, :] = bias
    bias_half = s.bias[0:1, cut]

    def activate_peer(at):
        r = pl.ds(at, CHUNK)
        low = pl.ds(pl.multiple_of(rows + at, CHUNK), CHUNK)
        value, slope = gelu_pair(s.pre[r, 0:half] + bias_half)
        s.acth[low, :] = value.astype(bf16)
        s.gpreh[low, :] = (s.gact_peer[r, :] * slope).astype(bf16)

    loop(rows, activate_peer)
    parts[0][...] = dot(s.acth[...], s.cots[...], 0, 0)
    send_up(range(NPIECES))
    sent[0] = NPIECES
    parts[1][...] = dot(s.h2[...], s.gpreh[...], 0, 0)
    send_up(range(NPIECES, 2 * NPIECES))
    sent[0] = 2 * NPIECES

    sum2.wait()

    def second_back(at, total):
        r = pl.ds(pl.multiple_of(own_rows + at, CHUNK), CHUNK)
        grad = sum2.rows(at, CHUNK)
        normed, inverse, _ = norm_forward(s.middle[pl.ds(at, CHUNK), :], gain2, shift2)
        mid = s.cot_f[r, :] + norm_backward(grad, normed, inverse, gain2)
        s.gmid[pl.ds(at, CHUNK), :] = mid
        s.wide[1][0][p.q, pl.ds(at, CHUNK), :] = mid.astype(bf16).astype(f32)
        terms = (grad * normed, grad, mid)
        return tuple(t + column_sum(v) for t, v in zip(total, terms))

    sums = loop(quarter, second_back, (jnp.zeros((1, width), f32),) * 3)
    for n, value in enumerate(sums):
        s.mine[3 + n : 4 + n, :] = value
    all2.start()
    s.sums[2][0][...] = dot(s.act[...], down_w[...], 1, 0).reshape(4, quarter, width)
    sum3.start()
    pump(3)
    all2.from_y()
    all2.from_x()
    all2.own_done()
    pump()
    s.gms[0:rows, :] = s.wide[1][0][...].reshape(rows, width).astype(bf16)
    sum3.first()
    sum3.second()
    for h in range(heads):
        get = lambda i: s.probs[h, i * BLOCK : (i + 1) * BLOCK, 0 : (i + 1) * BLOCK]
        head_back(h, 0, get, (1,))
    pump()
    one = dot(s.stack[0:rows, 0:local], attn_rows[0:local, :], 1, 0)
    for m in range(1, 3):
        item = s.stack[0:rows, m * 256 : m * 256 + local]
        one = one + dot(item, attn_rows[m * local : (m + 1) * local, :], 1, 0)
    s.sums[3][0][...] = one.reshape(4, quarter, width)
    sum4.start()
    pump()
    sum4.first()
    sum4.second()
    swap_tok.share()
    all2.from_diagonal()
    swap_tok.done()

    def peer_norm(at):
        low = pl.ds(pl.multiple_of(rows + at, CHUNK), CHUNK)
        t = s.tok_peer[pl.ds(at, CHUNK), :]
        s.hid1[low, :] = norm_forward(t, gain1, shift1)[2].astype(bf16)

    loop(rows, peer_norm)
    project(rows)
    pump()
    all2.peer_done()
    s.gms[rows:, :] = s.wide[1][1][...].reshape(rows, width).astype(bf16)
    note.wait_recv()
    length_peer = s.len_peer[0:1, 0:1]
    for h in range(heads):
        head_back(h, rows, lambda i: probabilities(h, i, length_peer), (1,))
    pump()

    left = s.stack[:, pl.ds(pl.multiple_of(p.x * 512, 128), local)]
    parts[2][0:local, :] = dot(left, s.hid1[...], 0, 0)

    @pl.when(p.x == 0)
    def _():
        parts[2][local:, :] = dot(s.stack[:, 256 : 256 + local], s.hid1[...], 0, 0)

    @pl.when(p.x == 1)
    def _():
        parts[2][local:, :] = dot(s.stack[:, 768 : 768 + local], s.gms[...], 0, 0)

    send_up(range(2 * NPIECES, count))
    sent[0] = count
    pump()
    sum4.wait()

    def first_back(row, total):
        r = pl.ds(pl.multiple_of(own_rows + row, CHUNK), CHUNK)
        grad = sum4.rows(row, CHUNK)
        normed, inverse, _ = norm_forward(s.tok_f[r, :], gain1, shift1)
        back = norm_backward(grad, normed, inverse, gain1)
        s.slim[1][0][p.q, pl.ds(row, CHUNK), :] = s.gmid[pl.ds(row, CHUNK), :] + back
        return tuple(t + column_sum(v) for t, v in zip(total, (grad * normed, grad)))

    sums = loop(quarter, first_back, (jnp.zeros((1, width), f32),) * 2)
    for n, value in enumerate(sums):
        s.mine[6 + n : 7 + n, :] = value
    all4.start()
    notes = []

    def note_out(value, device):
        n = len(notes)
        s.notes[n] = value
        notes.append(push(s.notes.at[n], s.heard.at[n], s.note_sem[0].at[n], s.note_sem[1].at[n], device))

    def note_in():
        notes[-1].wait_recv()
        return s.notes[len(notes) - 1] + s.heard[len(notes) - 1]

    note_out(s.mine[...], p.cn)
    pump()
    sum3.wait()
    bias = line(down_bias)

    def finish_block(row):
        full = s.middle[pl.ds(row, CHUNK), :] + sum3.rows(row, CHUNK) + bias
        valid = row_index(own_rows + row, CHUNK) < length
        s.slim[0][0][p.q, pl.ds(row, CHUNK), :] = jnp.where(valid, full, 0.0)

    loop(quarter, finish_block)
    all3.start()
    pump()
    note_out(note_in(), p.yn)
    pump(2)
    all4.from_y()
    all4.own_done()
    input_grad[...] = s.slim[1][0][...].reshape(rows, width).astype(bf16)
    which = lax.broadcasted_iota(jnp.int32, (8, width), 0)
    note_out(jnp.where(which < 3, s.mine[...], note_in()), p.xn)
    pump(2)
    all3.from_y()
    all3.own_done()
    block_out[...] = s.slim[0][0][...].reshape(rows, width).astype(bf16)
    note_out(note_in(), p.beside)
    pump(2)
    note_out(note_in(), p.mirror)
    pump(3)
    small_out[...] = note_in()

    while at[0] < count + EDGE_LAG:
        pump()
    for u in range(count):
        give(u).wait_recv()
    for job in (sum1, sum2, sum3, sum4, all1, all2, all3, all4, swap_cot, swap_tok):
        job.drain()
    for copy in [note] + notes:
        copy.wait_send()
    for u in range(count):
        give(u).wait_send()

    @pl.when(p.edge)
    def _():
        for u in range(count):
            up(u).wait_send()

    @pl.when(p.inner)
    def _():
        for u in range(count):
            cross(u).wait_send()
            down(u).wait_send()


def emit_kernel(*refs):
    (tile_a, tile_b, down, hidden, attn, small), outs, vecs, sem = refs[:6], refs[6:12], refs[12:21], refs[21]
    top = outs[2].shape[0]
    sources = [tile_a, tile_b, attn.at[pl.ds(0, top)], attn.at[pl.ds(top, outs[3].shape[0])], hidden, down]
    writes = [pltpu.make_async_copy(src, out, sem.at[n]) for n, (src, out) in enumerate(zip(sources, outs))]
    for write in writes:
        write.start()
    places = [(2, 0), (2, 256), (5, 0), (6, 0), (7, 0), (0, 0), (1, 0), (3, 0), (4, 0)]
    for ref, (row, lane) in zip(vecs, places):
        size = ref.shape[0]
        ref[...] = small[row : row + 1, lane : lane + size].reshape(size)
    for write in writes:
        write.wait()


def whole_block(operands):
    rows, width = operands[0].shape
    local = operands[3].shape[0] // 3
    hidden = operands[10].shape[1]
    f32 = jnp.float32
    scratch, tree = jax.tree.flatten(layout(operands))
    tile = jax.ShapeDtypeStruct((rows, width), jnp.bfloat16)
    mats = [(3 * local, width), (local, width), (width, hidden), (hidden, width)]
    vecs = [local, local, width, width, width, hidden, width, width, width]
    big = [tile, tile] + [jax.ShapeDtypeStruct(shape, f32) for shape in mats]
    held = [(tile.shape, tile.dtype)] * 2 + [(mats[3], f32), (mats[2], f32)]
    held += [((4 * local, width), f32), ((8, width), f32)]
    anywhere = pl.BlockSpec(memory_space=pl.ANY)
    results = pl.pallas_call(
        lambda *refs: block_kernel(tree, *refs),
        out_shape=[pltpu.VMEM(shape, kind) for shape, kind in held],
        in_specs=[anywhere] * len(operands),
        out_specs=[VM] * 6,
        scratch_shapes=scratch,
        compiler_params=pltpu.CompilerParams(
            collective_id=0, has_side_effects=True, vmem_limit_bytes=LIMIT
        ),
        name="whole_block",
    )(*operands)
    return pl.pallas_call(
        emit_kernel,
        out_shape=big + [jax.ShapeDtypeStruct((n,), f32) for n in vecs],
        in_specs=[VM] * 6,
        out_specs=[anywhere] * 6 + [VM] * 9,
        scratch_shapes=[pltpu.SemaphoreType.DMA((6,))],
        compiler_params=pltpu.CompilerParams(vmem_limit_bytes=4 * 1024 * 1024),
        name="emit",
    )(*results)


def plain_shards(
    tokens,
    segment_ids,
    cotangent,
    attn_input,
    query_bias,
    value_bias,
    attn_output,
    output_bias,
    gain_first,
    shift_first,
    hidden_weight,
    hidden_bias,
    down_weight,
    down_bias,
    gain_second,
    shift_second,
):
    row_count = tokens.shape[0]
    local_width = attn_input.shape[2]
    valid = (segment_ids >= 0)[:, None]
    cot_masked = jnp.where(valid, cotangent, jnp.zeros_like(cotangent))
    allowed = allowed_mask(segment_ids)
    resid_in = tokens.astype(jnp.float32)
    normed_one, inverse_one, pre_one = norm_forward(resid_in, gain_first, shift_first)
    hidden_one = pre_one.astype(jnp.bfloat16)
    projected = jnp.einsum(
        "rd,tdc->trc", hidden_one, attn_input, preferred_element_type=jnp.float32
    )
    queries = (projected[0] + query_bias).astype(jnp.bfloat16).reshape(row_count, -1, HD)
    keys_bf = projected[1].astype(jnp.bfloat16).reshape(row_count, -1, HD)
    values_bf = (projected[2] + value_bias).astype(jnp.bfloat16).reshape(row_count, -1, HD)
    mixed, log_sum = attend(queries, keys_bf, values_bf, allowed)
    attended = mixed.reshape(row_count, local_width).astype(jnp.bfloat16)
    attn_part = jnp.dot(attended, attn_output, preferred_element_type=jnp.float32)
    middle = resid_in + lax.psum(attn_part, "tensor") + output_bias
    normed_two, inverse_two, pre_two = norm_forward(middle, gain_second, shift_second)
    hidden_two = pre_two.astype(jnp.bfloat16)
    pre_act = jnp.dot(hidden_two, hidden_weight, preferred_element_type=jnp.float32) + hidden_bias
    gelu_value, gelu_slope = gelu_pair(pre_act)
    activation = gelu_value.astype(jnp.bfloat16)
    mlp_part = jnp.dot(activation, down_weight, preferred_element_type=jnp.float32)
    out_full = middle + lax.psum(mlp_part, "tensor") + down_bias
    block_out = jnp.where(valid, out_full, jnp.zeros_like(out_full)).astype(jnp.bfloat16)
    grad_top = cot_masked.astype(jnp.float32)
    grad_down_bias = jnp.sum(grad_top, axis=0)
    grad_down_weight = contract_rows(activation, cot_masked)
    grad_pre = contract_cols(cot_masked, down_weight) * gelu_slope
    grad_hidden_bias = jnp.sum(grad_pre, axis=0)
    grad_pre_bf = grad_pre.astype(jnp.bfloat16)
    grad_hidden_weight = contract_rows(hidden_two, grad_pre_bf)
    grad_two = lax.psum(contract_cols(grad_pre_bf, hidden_weight), "tensor")
    grad_gain_second = jnp.sum(grad_two * normed_two, axis=0)
    grad_shift_second = jnp.sum(grad_two, axis=0)
    grad_middle = grad_top + norm_backward(grad_two, normed_two, inverse_two, gain_second)
    grad_output_bias = jnp.sum(grad_middle, axis=0)
    grad_middle_bf = grad_middle.astype(jnp.bfloat16)
    grad_attn_output = contract_rows(attended, grad_middle_bf)
    grad_attended = (
        contract_cols(grad_middle_bf, attn_output).astype(jnp.bfloat16).reshape(row_count, -1, HD)
    )
    grad_queries, grad_keys, grad_values = attend_back(
        queries, keys_bf, values_bf, allowed, log_sum, grad_attended
    )
    grad_queries = grad_queries.reshape(row_count, local_width)
    grad_keys = grad_keys.reshape(row_count, local_width)
    grad_values = grad_values.reshape(row_count, local_width)
    grad_query_bias = jnp.sum(grad_queries, axis=0)
    grad_value_bias = jnp.sum(grad_values, axis=0)
    grad_stack = jnp.stack([grad_queries, grad_keys, grad_values]).astype(jnp.bfloat16)
    grad_attn_input = jnp.einsum(
        "rd,trc->tdc", hidden_one, grad_stack, preferred_element_type=jnp.float32
    )
    one_part = jnp.einsum("trc,tdc->rd", grad_stack, attn_input, preferred_element_type=jnp.float32)
    grad_one = lax.psum(one_part, "tensor")
    grad_gain_first = jnp.sum(grad_one * normed_one, axis=0)
    grad_shift_first = jnp.sum(grad_one, axis=0)
    input_grad = (
        grad_middle + norm_backward(grad_one, normed_one, inverse_one, gain_first)
    ).astype(jnp.bfloat16)
    (
        grad_attn_input,
        grad_query_bias,
        grad_value_bias,
        grad_attn_output,
        grad_output_bias,
        grad_gain_first,
        grad_shift_first,
        grad_hidden_weight,
        grad_hidden_bias,
        grad_down_weight,
        grad_down_bias,
        grad_gain_second,
        grad_shift_second,
    ) = lax.psum(
        (
            grad_attn_input,
            grad_query_bias,
            grad_value_bias,
            grad_attn_output,
            grad_output_bias,
            grad_gain_first,
            grad_shift_first,
            grad_hidden_weight,
            grad_hidden_bias,
            grad_down_weight,
            grad_down_bias,
            grad_gain_second,
            grad_shift_second,
        ),
        "dp",
    )
    return (
        block_out,
        input_grad,
        grad_attn_input,
        grad_query_bias,
        grad_value_bias,
        grad_attn_output,
        grad_output_bias,
        grad_gain_first,
        grad_shift_first,
        grad_hidden_weight,
        grad_hidden_bias,
        grad_down_weight,
        grad_down_bias,
        grad_gain_second,
        grad_shift_second,
    )


def shards(
    tokens,
    segment_ids,
    cotangent,
    attn_input,
    query_bias,
    value_bias,
    attn_output,
    output_bias,
    gain_first,
    shift_first,
    hidden_weight,
    hidden_bias,
    down_weight,
    down_bias,
    gain_second,
    shift_second,
):
    if lax.axis_size("tensor") != 4 or lax.axis_size("dp") != 8:
        return plain_shards(
            tokens,
            segment_ids,
            cotangent,
            attn_input,
            query_bias,
            value_bias,
            attn_output,
            output_bias,
            gain_first,
            shift_first,
            hidden_weight,
            hidden_bias,
            down_weight,
            down_bias,
            gain_second,
            shift_second,
        )
    local_width = attn_input.shape[2]
    width = tokens.shape[1]
    operands = (
        tokens,
        cotangent,
        segment_ids,
        attn_input.transpose(0, 2, 1).reshape(3 * local_width, width),
        query_bias,
        value_bias,
        attn_output,
        output_bias,
        gain_first,
        shift_first,
        hidden_weight,
        hidden_bias,
        down_weight,
        down_bias,
        gain_second,
        shift_second,
    )
    (
        block_out,
        input_grad,
        grad_in,
        grad_attn_output,
        grad_hidden_weight,
        grad_down_weight,
        grad_query_bias,
        grad_value_bias,
        grad_output_bias,
        grad_gain_first,
        grad_shift_first,
        grad_hidden_bias,
        grad_down_bias,
        grad_gain_second,
        grad_shift_second,
    ) = whole_block(operands)
    return (
        block_out,
        input_grad,
        grad_in.reshape(3, local_width, width).transpose(0, 2, 1),
        grad_query_bias,
        grad_value_bias,
        grad_attn_output,
        grad_output_bias,
        grad_gain_first,
        grad_shift_first,
        grad_hidden_weight,
        grad_hidden_bias,
        grad_down_weight,
        grad_down_bias,
        grad_gain_second,
        grad_shift_second,
    )


def solution(mesh):
    return jax.shard_map(
        shards,
        mesh=mesh,
        in_specs=(
            P("dp", None),
            P("dp"),
            P("dp", None),
            P(None, None, "tensor"),
            P("tensor"),
            P("tensor"),
            P("tensor", None),
            P(),
            P(),
            P(),
            P(None, "tensor"),
            P("tensor"),
            P("tensor", None),
            P(),
            P(),
            P(),
        ),
        out_specs=(
            P("dp", None),
            P("dp", None),
            P(None, None, "tensor"),
            P("tensor"),
            P("tensor"),
            P("tensor", None),
            P(),
            P(),
            P(),
            P(None, "tensor"),
            P("tensor"),
            P("tensor", None),
            P(),
            P(),
            P(),
        ),
        check_vma=False,
    )
```

```python
import types

import jax
import jax.numpy as jnp
from jax import lax
from jax.experimental import pallas as pl
from jax.experimental.pallas import tpu as pltpu
from jax.sharding import PartitionSpec as P

HD = 64
MESH = pl.DeviceIdType.MESH
VM = pl.BlockSpec(memory_space=pltpu.VMEM)


EPSILON = 1e-05
TANH_SCALE = 0.7978845608028654
CUBIC = 0.044715


def norm_forward(values_in, norm_gain, norm_shift):
    row_mean = jnp.mean(values_in, axis=-1, keepdims=True)
    centered = values_in - row_mean
    inverse = lax.rsqrt(jnp.mean(centered * centered, axis=-1, keepdims=True) + EPSILON)
    normed = centered * inverse
    return (normed, inverse, normed * norm_gain + norm_shift)


def norm_backward(grad_out, normed, inverse, norm_gain):
    scaled = grad_out * norm_gain
    return inverse * (
        scaled
        - jnp.mean(scaled, axis=-1, keepdims=True)
        - normed * jnp.mean(scaled * normed, axis=-1, keepdims=True)
    )


def gelu_pair(pre_act):
    tangent = jnp.tanh(TANH_SCALE * (pre_act + CUBIC * pre_act * pre_act * pre_act))
    gelu_value = 0.5 * pre_act * (1.0 + tangent)
    gelu_slope = 0.5 * (1.0 + tangent) + 0.5 * pre_act * (1.0 - tangent * tangent) * TANH_SCALE * (
        1.0 + 3.0 * CUBIC * pre_act * pre_act
    )
    return (gelu_value, gelu_slope)


def contract_rows(left_mat, right_mat):
    return lax.dot_general(
        left_mat, right_mat, (((0,), (0,)), ((), ())), preferred_element_type=jnp.float32
    )


def contract_cols(left_mat, right_mat):
    return lax.dot_general(
        left_mat, right_mat, (((1,), (1,)), ((), ())), preferred_element_type=jnp.float32
    )


def allowed_mask(segments):
    position = jnp.arange(segments.shape[0])
    return (segments[:, None] == segments[None, :]) & (position[None, :] <= position[:, None])


def head_scores(queries, keys_bf, allowed):
    scaling = queries.shape[-1] ** (-0.5)
    scores = (
        jnp.einsum("qhd,khd->hqk", queries, keys_bf, preferred_element_type=jnp.float32) * scaling
    )
    return jnp.where(allowed[None], scores, -jnp.inf)


def attend(queries, keys_bf, values_bf, allowed):
    scores = head_scores(queries, keys_bf, allowed)
    top_score = jnp.max(scores, axis=-1, keepdims=True)
    log_sum = top_score + jnp.log(jnp.sum(jnp.exp(scores - top_score), axis=-1, keepdims=True))
    probs = jnp.exp(scores - log_sum).astype(jnp.bfloat16)
    mixed = jnp.einsum("hqk,khd->qhd", probs, values_bf, preferred_element_type=jnp.float32)
    return (mixed, log_sum)


def attend_back(queries, keys_bf, values_bf, allowed, log_sum, grad_mixed):
    probs_full = jnp.exp(head_scores(queries, keys_bf, allowed) - log_sum)
    probs_bf = probs_full.astype(jnp.bfloat16)
    grad_values = jnp.einsum(
        "hqk,qhd->khd", probs_bf, grad_mixed, preferred_element_type=jnp.float32
    )
    grad_probs = jnp.einsum(
        "qhd,khd->hqk", grad_mixed, values_bf, preferred_element_type=jnp.float32
    )
    scaling = queries.shape[-1] ** (-0.5)
    grad_scores = (
        probs_full
        * (grad_probs - jnp.sum(probs_full * grad_probs, axis=-1, keepdims=True))
        * scaling
    ).astype(jnp.bfloat16)
    grad_queries = jnp.einsum(
        "hqk,khd->qhd", grad_scores, keys_bf, preferred_element_type=jnp.float32
    )
    grad_keys = jnp.einsum("hqk,qhd->khd", grad_scores, queries, preferred_element_type=jnp.float32)
    return (grad_queries, grad_keys, grad_values)


CHUNK = 48
BLOCK = 128
NPIECES = 8
LAG = 2
EDGE_LAG = 3
LIMIT = 55 * 1024 * 1024


def dot(left, right, left_dim, right_dim):
    return lax.dot_general(
        left, right, (((left_dim,), (right_dim,)), ((), ())), preferred_element_type=jnp.float32
    )


def remote(src, dst, send, recv, device):
    return pltpu.make_async_remote_copy(
        src_ref=src,
        dst_ref=dst,
        send_sem=send,
        recv_sem=recv,
        device_id=device,
        device_id_type=MESH,
    )


def push(src, dst, send, recv, device):
    copy = remote(src, dst, send, recv, device)
    copy.start()
    return copy


def greet(peers):
    barrier = pltpu.get_barrier_semaphore()
    for peer in peers:
        pl.semaphore_signal(barrier, inc=1, device_id=peer, device_id_type=MESH)
    pl.semaphore_wait(barrier, len(peers))


class Place:
    def __init__(self):
        dp = self.dp = lax.axis_index("dp")
        me = self.me = lax.axis_index("tensor")
        x = self.x = dp % 2
        line = dp // 2
        y, k = me // 2, me % 2
        self.k = k
        self.inner = (line == 1) | (line == 2)
        self.edge = (line == 0) | (line == 3)
        odd = line % 2
        self.xn = (dp + 1 - 2 * x, me)
        self.yn = (dp, (me + 2) % 4)
        self.cn = (dp, me + 1 - 2 * k)
        self.beside = ((line + 1 - 2 * odd) * 2 + x, me)
        self.mirror = ((3 - line) * 2 + x, me)
        self.q = k * 2 + y
        self.qy = k * 2 + 1 - y
        self.qc = (1 - k) * 2 + y
        self.qcy = (1 - k) * 2 + 1 - y


class Reduce:
    def __init__(self, place, part, rx, mid, ry, send, recv):
        self.p, self.part, self.rx, self.mid, self.ry = place, part, rx, mid, ry
        self.send, self.recv = send, recv

    def start(self):
        p = self.p
        self.c = [
            push(self.part.at[p.qcy], self.rx.at[0], self.send.at[0], self.recv.at[0], p.cn),
            push(self.part.at[p.qc], self.rx.at[1], self.send.at[1], self.recv.at[1], p.cn),
        ]

    def first(self):
        p = self.p
        self.c[0].wait_recv()
        self.mid[...] = self.part[p.qy] + self.rx[0]
        self.c.append(push(self.mid, self.ry, self.send.at[2], self.recv.at[2], p.yn))

    def second(self):
        self.c[1].wait_recv()
        self.rx[1] = self.part[self.p.q] + self.rx[1]

    def wait(self):
        self.c[2].wait_recv()

    def rows(self, at, size):
        return self.rx[1, pl.ds(at, size), :] + self.ry[pl.ds(at, size), :]

    def drain(self):
        for copy in self.c:
            copy.wait_send()


class Gather:
    def __init__(self, place, own, peer, send, recv):
        self.p, self.own, self.peer, self.send, self.recv = place, own, peer, send, recv
        self.c = {}

    def go(self, n, ref, at, device, into=None):
        into = ref if into is None else into
        self.c[n] = push(ref.at[at], into.at[at], self.send.at[n], self.recv.at[n], device)

    def start(self):
        p = self.p
        self.go(0, self.own, p.q, p.yn)
        self.go(3, self.own, p.q, p.cn)
        if self.peer is not None:
            self.go(1, self.own, p.q, p.xn, self.peer)

    def from_y(self):
        self.c[0].wait_recv()
        self.go(4, self.own, self.p.qy, self.p.cn)
        if self.peer is not None:
            self.slip(7, self.own, self.p.qy, 0, self.p.xn)

    def own_done(self):
        self.c[3].wait_recv()
        self.c[4].wait_recv()

    def from_x(self):
        self.c[1].wait_recv()
        self.slip(2, self.peer, self.p.q, 1, self.p.yn)
        self.go(5, self.peer, self.p.q, self.p.cn)

    def slip(self, n, ref, at, part, device):
        size = ref.shape[1] // 2
        rows = pl.ds(part * size, size)
        src, into = ref.at[at, rows], self.peer.at[at, rows]
        self.c[n] = push(src, into, self.send.at[n], self.recv.at[n], device)

    def from_diagonal(self):
        self.c[2].wait_recv()
        self.c[7].wait_recv()
        self.go(6, self.peer, self.p.qy, self.p.cn)

    def peer_done(self):
        self.c[5].wait_recv()
        self.c[6].wait_recv()

    def drain(self):
        for copy in self.c.values():
            copy.wait_send()


class Swap:
    def __init__(self, place, src, dst, send, recv):
        self.p, self.src, self.dst, self.send, self.recv = place, src, dst, send, recv
        half = src.shape[0] // 2
        self.rows = pl.ds(pl.multiple_of(place.k * half, 8), half)

    def start(self):
        src, dst = self.src.at[self.rows], self.dst.at[self.rows]
        self.c = [push(src, dst, self.send.at[0], self.recv.at[0], self.p.xn)]

    def share(self):
        self.c[0].wait_recv()
        dst = self.dst.at[self.rows]
        self.c.append(push(dst, dst, self.send.at[1], self.recv.at[1], self.p.cn))

    def done(self):
        self.c[1].wait_recv()

    def drain(self):
        for copy in self.c:
            copy.wait_send()


def layout(operands):
    rows, width = operands[0].shape
    local, hidden = operands[3].shape[0] // 3, operands[10].shape[1]
    heads, quarter, half = local // HD, rows // 4, hidden // 2
    f32, bf16 = jnp.float32, jnp.bfloat16
    b = types.SimpleNamespace()
    b.args = [pltpu.VMEM(item.shape, item.dtype) for item in operands]
    b.arg_sem = pltpu.SemaphoreType.DMA((len(operands),))

    def mem(*shape, kind=f32):
        return pltpu.VMEM(shape, kind)

    def sems(count):
        return [pltpu.SemaphoreType.DMA((count,))] * 2

    b.tok_f, b.cot_f = mem(rows, width), mem(rows, width)
    b.tok_peer, b.cot_peer = [mem(rows, width)] * 2
    b.swaps = [sems(2)] * 2
    b.len_own, b.len_peer, b.len_sem = mem(8, 128), mem(8, 128), sems(1)
    b.hid1, b.h2, b.cots, b.gms = [mem(2 * rows, width, kind=bf16)] * 4
    b.stack = mem(2 * rows, 4 * 256, kind=bf16)
    b.acth, b.gpreh = [mem(2 * rows, half, kind=bf16)] * 2
    b.act, b.gpre = [mem(rows, hidden, kind=bf16)] * 2
    b.pre, b.gact, b.gact_peer = mem(rows, hidden), mem(rows, hidden), mem(rows, half)
    b.probs = mem(heads, rows, rows)
    b.heads = mem(3 * heads, rows, HD, kind=bf16)
    b.gk, b.gv = mem(rows, HD), mem(rows, HD)
    four, two, one = mem(4, quarter, width), mem(2, quarter, width), mem(quarter, width)
    b.sums = [[four, two, one, one, *sems(3)]] * 4
    b.wide = [[four, four, *sems(8)]] * 2
    b.slim = [[four, *sems(7)]] * 2
    b.middle, b.gmid = one, one
    b.parts = [mem(half, width), mem(width, half), mem(2 * local, width)]
    cut = [(x.shape[0] // NPIECES, x.shape[1]) for x in b.parts]
    b.rz = [mem(NPIECES, *shape) for shape in cut]
    b.ry = [mem(NPIECES, *shape) for shape in cut]
    b.up, b.cross, b.down, b.give = [sems(3 * NPIECES)] * 4
    b.bias, b.mine = mem(8, hidden), mem(8, width)
    b.notes, b.heard, b.note_sem = mem(5, 8, width), mem(5, 8, width), sems(5)
    return vars(b)


def loop(rows, body, init=None, size=CHUNK):
    if init is None:

        def run(i, _):
            body(pl.multiple_of(i * size, size))
            return 0

        lax.fori_loop(0, rows // size, run, 0)
        return None
    return lax.fori_loop(0, rows // size, lambda i, c: body(pl.multiple_of(i * size, size), c), init)


def column_sum(values):
    return jnp.sum(values, axis=0, keepdims=True)


def block_kernel(tree, *refs):
    block_out, input_grad = refs[16:18]
    tots, small_out = refs[18:21], refs[21]
    s = types.SimpleNamespace(**jax.tree.unflatten(tree, refs[22:]))
    (tokens, cot, seg, attn_rows, query_bias, value_bias, attn_output, output_bias) = s.args[:8]
    (gain_one, shift_one, hidden_w, hidden_bias, down_w, down_bias, gain_two, shift_two) = s.args[8:]
    loads = [pltpu.make_async_copy(refs[n], s.args[n], s.arg_sem.at[n]) for n in range(16)]
    for n in (2, 1, 0, 8, 9, 3, 4, 5, 6, 7, 14, 15, 12, 10, 11, 13):
        loads[n].start()

    def ready(*which):
        for n in which:
            loads[n].wait()
    f32, bf16 = jnp.float32, jnp.bfloat16
    rows, width = tokens.shape
    local = attn_rows.shape[0] // 3
    hidden = hidden_w.shape[1]
    heads, quarter, half = local // HD, rows // 4, hidden // 2
    p = Place()

    def line(ref):
        return ref[...].reshape(1, ref.shape[0])

    sum1, sum2, sum3, sum4 = (Reduce(p, *item) for item in s.sums)
    all1, all2 = (Gather(p, *item) for item in s.wide)
    all3, all4 = (Gather(p, own, None, *rest) for own, *rest in s.slim)
    swap_cot = Swap(p, s.cot_f, s.cot_peer, *s.swaps[0])
    swap_tok = Swap(p, s.tok_f, s.tok_peer, *s.swaps[1])

    parts, rz, ry = s.parts, s.rz, s.ry
    units = [(m, i) for m in range(3) for i in range(NPIECES)]
    count = len(units)

    def piece(u):
        m, i = units[u]
        size = parts[m].shape[0] // NPIECES
        return parts[m].at[pl.ds(i * size, size)]

    def place_of(u, column):
        m, i = units[u]
        tall, wide = parts[m].shape
        size = tall // NPIECES
        if m == 1:
            return tots[m].at[pl.ds(i * size, size), pl.ds(pl.multiple_of(column * wide, 128), wide)]
        return tots[m].at[pl.ds(pl.multiple_of(column * tall + i * size, 8), size)]

    def hop(sem, src, dst, u, device):
        return remote(src, dst, sem[0].at[u], sem[1].at[u], device)

    def up(u):
        m, i = units[u]
        return hop(s.up, piece(u), rz[m].at[i], u, p.beside)

    def cross(u):
        m, i = units[u]
        return hop(s.cross, piece(u), ry[m].at[i], u, p.mirror)

    def down(u):
        return hop(s.down, place_of(u, p.x), place_of(u, p.x), u, p.beside)

    def give(u):
        return hop(s.give, place_of(u, p.x), place_of(u, p.x), u, p.xn)

    def send_up(us):
        @pl.when(p.edge)
        def _():
            for u in us:
                up(u).start()

    def step(at):
        @pl.when(p.inner)
        def _():
            if at < count:
                m, i = units[at]
                up(at).wait_recv()
                src = piece(at)
                src[...] = src[...] + rz[m][i]
                cross(at).start()
            if 0 <= at - LAG < count:
                u = at - LAG
                m, i = units[u]
                cross(u).wait_recv()
                place_of(u, p.x)[...] = piece(u)[...] + ry[m][i]
                down(u).start()
                give(u).start()

        if 0 <= at - EDGE_LAG < count:

            @pl.when(p.edge)
            def _():
                down(at - EDGE_LAG).wait_recv()
                give(at - EDGE_LAG).start()

    at, sent = [0], [0]

    def pump(n=1):
        for _ in range(n):
            if at[0] < sent[0] or sent[0] == count:
                step(at[0])
                at[0] += 1

    greet([p.xn, p.yn, p.cn, p.beside, p.mirror])
    ready(1, 2)
    inside = jnp.where(line(seg) >= 0, 1.0, 0.0)
    length = jnp.sum(inside, axis=1, keepdims=True)
    s.len_own[...] = jnp.broadcast_to(length, (8, 128))
    note = push(s.len_own, s.len_peer, s.len_sem[0].at[0], s.len_sem[1].at[0], p.xn)

    def row_index(at, size):
        return (lax.broadcasted_iota(jnp.int32, (size, 1), 0) + at).astype(f32)

    def masked(at):
        keep = row_index(at, CHUNK) < length
        return jnp.where(keep, cot[pl.ds(at, CHUNK), :].astype(f32), 0.0)

    def mask_half(at):
        at = pl.multiple_of(p.k * (rows // 2) + at, CHUNK)
        s.cot_f[pl.ds(at, CHUNK), :] = masked(at)

    def mask_cot(at, total):
        values = masked(at)
        s.cots[pl.ds(at, CHUNK), :] = values.astype(bf16)
        return total + column_sum(values)

    loop(rows // 2, mask_half)
    swap_cot.start()
    ready(0, 8, 9)
    gain1, shift1 = line(gain_one), line(shift_one)

    def first_norm(at):
        t = tokens[pl.ds(at, CHUNK), :].astype(f32)
        s.tok_f[pl.ds(at, CHUNK), :] = t
        s.hid1[pl.ds(at, CHUNK), :] = norm_forward(t, gain1, shift1)[2].astype(bf16)

    loop(rows, first_norm)

    def project(base):
        normal = s.hid1[base : base + rows, :]
        for m in range(3):
            out = dot(normal, attn_rows[m * local : (m + 1) * local, :], 1, 1)
            if m == 0:
                out = (out + line(query_bias)).astype(bf16) * jnp.asarray(HD ** (-0.5), bf16)
            elif m == 1:
                out = out.astype(bf16)
            else:
                out = (out + line(value_bias)).astype(bf16)
            for h in range(heads):
                s.heads[m * heads + h] = out[:, h * HD : (h + 1) * HD]

    def probabilities(h, i, bound):
        top_row, n = i * BLOCK, (i + 1) * BLOCK
        query = s.heads[h, top_row:n, :]
        key = s.heads[heads + h, 0:n, :]
        row = (lax.broadcasted_iota(jnp.int32, (BLOCK, n), 0) + top_row).astype(f32)
        col = lax.broadcasted_iota(jnp.int32, (BLOCK, n), 1).astype(f32)
        allowed = (col <= row) & ((col >= bound) | (row < bound))
        scores = jnp.where(allowed, dot(query, key, 1, 1), -jnp.inf)
        e = jnp.exp(scores - jnp.max(scores, axis=1, keepdims=True))
        return e * (1.0 / jnp.sum(e, axis=1, keepdims=True))

    def mix(h, i, base, probs_bf):
        n = (i + 1) * BLOCK
        value = s.heads[2 * heads + h, 0:n, :]
        mixed = dot(probs_bf, value, 1, 0).astype(bf16)
        at = 3 * 256 + h * HD
        s.stack[base + i * BLOCK : base + n, at : at + HD] = mixed

    def head_back(h, base, get, beats):
        blocks = rows // BLOCK
        sums = []

        def only(x, body):
            if base:
                pl.when(p.x == x)(body)
            else:
                body()

        def into(ref, n, value, first):
            if first:
                ref[...] = value
            else:
                ref[0:n, :] += value

        for i in reversed(range(blocks)):
            if i in beats:
                pump()
            top_row, n = i * BLOCK, (i + 1) * BLOCK
            r = slice(base + top_row, base + n)
            probs = get(i)
            mixed = dot(s.gms[r, :], attn_output[h * HD : (h + 1) * HD, :], 1, 1).astype(bf16)

            def values():
                probs_bf = probs.astype(bf16)
                if base:
                    mix(h, i, base, probs_bf)
                into(s.gv, n, dot(probs_bf, mixed, 0, 0), i == blocks - 1)

            def scores():
                value = s.heads[2 * heads + h, 0:n, :]
                key = s.heads[heads + h, 0:n, :]
                grad_probs = dot(mixed, value, 1, 1)
                weighted = jnp.sum(probs * grad_probs, axis=1, keepdims=True)
                grad = (probs * (grad_probs - weighted)).astype(bf16)
                query = s.heads[h, top_row:n, :]
                grad_query = dot(grad, key, 1, 0) * HD ** (-0.5)
                into(s.gk, n, dot(grad, query, 0, 0), i == blocks - 1)
                s.stack[r, h * HD : (h + 1) * HD] = grad_query.astype(bf16)
                if not base:
                    sums.append(column_sum(grad_query))

            only(0, scores)
            only(1, values)

        def store(at, ref):
            s.stack[base : base + rows, at + h * HD : at + (h + 1) * HD] = ref[...].astype(bf16)

        only(0, lambda: store(256, s.gk))
        only(1, lambda: store(512, s.gv))
        if not base:
            s.mine[2:3, h * HD : (h + 1) * HD] = sum(sums[1:], sums[0])
            s.mine[2:3, 256 + h * HD : 256 + (h + 1) * HD] = column_sum(s.gv[...])

    ready(3, 4, 5)
    project(0)
    ready(6)
    for h in range(heads):
        for i in range(rows // BLOCK):
            n = (i + 1) * BLOCK
            probs = probabilities(h, i, length)
            s.probs[h, i * BLOCK : n, 0:n] = probs
            mix(h, i, 0, probs.astype(bf16))
    attended = s.stack[0:rows, 3 * 256 : 3 * 256 + local]
    s.sums[0][0][...] = dot(attended, attn_output[...], 1, 0).reshape(4, quarter, width)
    sum1.start()
    sum1.first()
    sum1.second()
    s.mine[...] = jnp.zeros_like(s.mine)
    s.mine[1:2, :] = loop(rows, mask_cot, jnp.zeros((1, width), f32))
    ready(7, 14, 15, 12)
    gain2, shift2 = line(gain_two), line(shift_two)
    s.gact[...] = dot(s.cots[0:rows, :], down_w[...], 1, 1)

    own_rows = p.q * quarter
    out_bias = line(output_bias)
    sum1.wait()

    def second_norm(at):
        r = pl.ds(pl.multiple_of(own_rows + at, CHUNK), CHUNK)
        middle = s.tok_f[r, :] + sum1.rows(at, CHUNK) + out_bias
        s.middle[pl.ds(at, CHUNK), :] = middle
        normal = norm_forward(middle, gain2, shift2)[2].astype(bf16)
        s.wide[0][0][p.q, pl.ds(at, CHUNK), :] = normal.astype(f32)

    loop(quarter, second_norm)
    all1.start()
    ready(10, 11, 13)
    cut = pl.ds(pl.multiple_of(p.x * half, 128), half)
    swap_cot.share()
    swap_cot.done()
    s.cots[rows:, :] = s.cot_peer[...].astype(bf16)
    s.gact_peer[...] = dot(s.cots[rows:, :], down_w[cut, :], 1, 1)
    all1.from_y()
    all1.from_x()
    swap_tok.start()
    all1.own_done()

    s.h2[0:rows, :] = s.wide[0][0][...].reshape(rows, width).astype(bf16)
    s.pre[...] = dot(s.h2[0:rows, :], hidden_w[...], 1, 0)
    bias = line(hidden_bias)

    def activate(at, total):
        r = pl.ds(at, CHUNK)
        value, slope = gelu_pair(s.pre[r, :] + bias)
        s.act[r, :] = value.astype(bf16)
        grad = s.gact[r, :] * slope
        s.gpre[r, :] = grad.astype(bf16)
        return total + column_sum(grad)

    s.mine[0:1, :] = loop(rows, activate, jnp.zeros((1, hidden), f32))
    s.sums[1][0][...] = dot(s.gpre[...], hidden_w[...], 1, 1).reshape(4, quarter, width)
    sum2.start()
    sum2.first()
    sum2.second()
    s.acth[0:rows, :] = s.act[:, cut]
    s.gpreh[0:rows, :] = s.gpre[:, cut]

    all1.from_diagonal()
    all1.peer_done()
    s.h2[rows:, :] = s.wide[0][1][...].reshape(rows, width).astype(bf16)
    s.pre[:, 0:half] = dot(s.h2[rows:, :], hidden_w[:, cut], 1, 0)
    s.bias[0:1, :] = bias
    bias_half = s.bias[0:1, cut]

    def activate_peer(at):
        r = pl.ds(at, CHUNK)
        low = pl.ds(pl.multiple_of(rows + at, CHUNK), CHUNK)
        value, slope = gelu_pair(s.pre[r, 0:half] + bias_half)
        s.acth[low, :] = value.astype(bf16)
        s.gpreh[low, :] = (s.gact_peer[r, :] * slope).astype(bf16)

    loop(rows, activate_peer)
    parts[0][...] = dot(s.acth[...], s.cots[...], 0, 0)
    send_up(range(NPIECES))
    sent[0] = NPIECES
    parts[1][...] = dot(s.h2[...], s.gpreh[...], 0, 0)
    send_up(range(NPIECES, 2 * NPIECES))
    sent[0] = 2 * NPIECES

    sum2.wait()

    def second_back(at, total):
        r = pl.ds(pl.multiple_of(own_rows + at, CHUNK), CHUNK)
        grad = sum2.rows(at, CHUNK)
        normed, inverse, _ = norm_forward(s.middle[pl.ds(at, CHUNK), :], gain2, shift2)
        mid = s.cot_f[r, :] + norm_backward(grad, normed, inverse, gain2)
        s.gmid[pl.ds(at, CHUNK), :] = mid
        s.wide[1][0][p.q, pl.ds(at, CHUNK), :] = mid.astype(bf16).astype(f32)
        terms = (grad * normed, grad, mid)
        return tuple(t + column_sum(v) for t, v in zip(total, terms))

    sums = loop(quarter, second_back, (jnp.zeros((1, width), f32),) * 3)
    for n, value in enumerate(sums):
        s.mine[3 + n : 4 + n, :] = value
    all2.start()
    s.sums[2][0][...] = dot(s.act[...], down_w[...], 1, 0).reshape(4, quarter, width)
    sum3.start()
    pump(3)
    all2.from_y()
    all2.from_x()
    all2.own_done()
    pump()
    s.gms[0:rows, :] = s.wide[1][0][...].reshape(rows, width).astype(bf16)
    sum3.first()
    sum3.second()
    for h in range(heads):
        get = lambda i: s.probs[h, i * BLOCK : (i + 1) * BLOCK, 0 : (i + 1) * BLOCK]
        head_back(h, 0, get, (1,))
    pump()
    one = dot(s.stack[0:rows, 0:local], attn_rows[0:local, :], 1, 0)
    for m in range(1, 3):
        item = s.stack[0:rows, m * 256 : m * 256 + local]
        one = one + dot(item, attn_rows[m * local : (m + 1) * local, :], 1, 0)
    s.sums[3][0][...] = one.reshape(4, quarter, width)
    sum4.start()
    pump()
    sum4.first()
    sum4.second()
    swap_tok.share()
    all2.from_diagonal()
    swap_tok.done()

    def peer_norm(at):
        low = pl.ds(pl.multiple_of(rows + at, CHUNK), CHUNK)
        t = s.tok_peer[pl.ds(at, CHUNK), :]
        s.hid1[low, :] = norm_forward(t, gain1, shift1)[2].astype(bf16)

    loop(rows, peer_norm)
    project(rows)
    pump()
    all2.peer_done()
    s.gms[rows:, :] = s.wide[1][1][...].reshape(rows, width).astype(bf16)
    note.wait_recv()
    length_peer = s.len_peer[0:1, 0:1]
    for h in range(heads):
        head_back(h, rows, lambda i: probabilities(h, i, length_peer), (1,))
    pump()

    left = s.stack[:, pl.ds(pl.multiple_of(p.x * 512, 128), local)]
    parts[2][0:local, :] = dot(left, s.hid1[...], 0, 0)

    @pl.when(p.x == 0)
    def _():
        parts[2][local:, :] = dot(s.stack[:, 256 : 256 + local], s.hid1[...], 0, 0)

    @pl.when(p.x == 1)
    def _():
        parts[2][local:, :] = dot(s.stack[:, 768 : 768 + local], s.gms[...], 0, 0)

    send_up(range(2 * NPIECES, count))
    sent[0] = count
    pump()
    sum4.wait()

    def first_back(row, total):
        r = pl.ds(pl.multiple_of(own_rows + row, CHUNK), CHUNK)
        grad = sum4.rows(row, CHUNK)
        normed, inverse, _ = norm_forward(s.tok_f[r, :], gain1, shift1)
        back = norm_backward(grad, normed, inverse, gain1)
        s.slim[1][0][p.q, pl.ds(row, CHUNK), :] = s.gmid[pl.ds(row, CHUNK), :] + back
        return tuple(t + column_sum(v) for t, v in zip(total, (grad * normed, grad)))

    sums = loop(quarter, first_back, (jnp.zeros((1, width), f32),) * 2)
    for n, value in enumerate(sums):
        s.mine[6 + n : 7 + n, :] = value
    all4.start()
    notes = []

    def note_out(value, device):
        n = len(notes)
        s.notes[n] = value
        notes.append(push(s.notes.at[n], s.heard.at[n], s.note_sem[0].at[n], s.note_sem[1].at[n], device))

    def note_in():
        notes[-1].wait_recv()
        return s.notes[len(notes) - 1] + s.heard[len(notes) - 1]

    note_out(s.mine[...], p.cn)
    pump()
    sum3.wait()
    bias = line(down_bias)

    def finish_block(row):
        full = s.middle[pl.ds(row, CHUNK), :] + sum3.rows(row, CHUNK) + bias
        valid = row_index(own_rows + row, CHUNK) < length
        s.slim[0][0][p.q, pl.ds(row, CHUNK), :] = jnp.where(valid, full, 0.0)

    loop(quarter, finish_block)
    all3.start()
    pump()
    note_out(note_in(), p.yn)
    pump(2)
    all4.from_y()
    all4.own_done()
    input_grad[...] = s.slim[1][0][...].reshape(rows, width).astype(bf16)
    which = lax.broadcasted_iota(jnp.int32, (8, width), 0)
    note_out(jnp.where(which < 3, s.mine[...], note_in()), p.xn)
    pump(2)
    all3.from_y()
    all3.own_done()
    block_out[...] = s.slim[0][0][...].reshape(rows, width).astype(bf16)
    note_out(note_in(), p.beside)
    pump(2)
    note_out(note_in(), p.mirror)
    pump(3)
    small_out[...] = note_in()

    while at[0] < count + EDGE_LAG:
        pump()
    for u in range(count):
        give(u).wait_recv()
    for job in (sum1, sum2, sum3, sum4, all1, all2, all3, all4, swap_cot, swap_tok):
        job.drain()
    for copy in [note] + notes:
        copy.wait_send()
    for u in range(count):
        give(u).wait_send()

    @pl.when(p.edge)
    def _():
        for u in range(count):
            up(u).wait_send()

    @pl.when(p.inner)
    def _():
        for u in range(count):
            cross(u).wait_send()
            down(u).wait_send()


def emit_kernel(*refs):
    (tile_a, tile_b, down, hidden, attn, small), outs, vecs, sem = refs[:6], refs[6:12], refs[12:21], refs[21]
    top = outs[2].shape[0]
    sources = [tile_a, tile_b, attn.at[pl.ds(0, top)], attn.at[pl.ds(top, outs[3].shape[0])], hidden, down]
    writes = [pltpu.make_async_copy(src, out, sem.at[n]) for n, (src, out) in enumerate(zip(sources, outs))]
    for write in writes:
        write.start()
    places = [(2, 0), (2, 256), (5, 0), (6, 0), (7, 0), (0, 0), (1, 0), (3, 0), (4, 0)]
    for ref, (row, lane) in zip(vecs, places):
        size = ref.shape[0]
        ref[...] = small[row : row + 1, lane : lane + size].reshape(size)
    for write in writes:
        write.wait()


def whole_block(operands):
    rows, width = operands[0].shape
    local = operands[3].shape[0] // 3
    hidden = operands[10].shape[1]
    f32 = jnp.float32
    scratch, tree = jax.tree.flatten(layout(operands))
    tile = jax.ShapeDtypeStruct((rows, width), jnp.bfloat16)
    mats = [(3 * local, width), (local, width), (width, hidden), (hidden, width)]
    vecs = [local, local, width, width, width, hidden, width, width, width]
    big = [tile, tile] + [jax.ShapeDtypeStruct(shape, f32) for shape in mats]
    held = [(tile.shape, tile.dtype)] * 2 + [(mats[3], f32), (mats[2], f32)]
    held += [((4 * local, width), f32), ((8, width), f32)]
    anywhere = pl.BlockSpec(memory_space=pl.ANY)
    results = pl.pallas_call(
        lambda *refs: block_kernel(tree, *refs),
        out_shape=[pltpu.VMEM(shape, kind) for shape, kind in held],
        in_specs=[anywhere] * len(operands),
        out_specs=[VM] * 6,
        scratch_shapes=scratch,
        compiler_params=pltpu.CompilerParams(
            collective_id=0, has_side_effects=True, vmem_limit_bytes=LIMIT
        ),
        name="whole_block",
    )(*operands)
    return pl.pallas_call(
        emit_kernel,
        out_shape=big + [jax.ShapeDtypeStruct((n,), f32) for n in vecs],
        in_specs=[VM] * 6,
        out_specs=[anywhere] * 6 + [VM] * 9,
        scratch_shapes=[pltpu.SemaphoreType.DMA((6,))],
        compiler_params=pltpu.CompilerParams(vmem_limit_bytes=4 * 1024 * 1024),
        name="emit",
    )(*results)


def plain_shards(
    tokens,
    segment_ids,
    cotangent,
    attn_input,
    query_bias,
    value_bias,
    attn_output,
    output_bias,
    gain_first,
    shift_first,
    hidden_weight,
    hidden_bias,
    down_weight,
    down_bias,
    gain_second,
    shift_second,
):
    row_count = tokens.shape[0]
    local_width = attn_input.shape[2]
    valid = (segment_ids >= 0)[:, None]
    cot_masked = jnp.where(valid, cotangent, jnp.zeros_like(cotangent))
    allowed = allowed_mask(segment_ids)
    resid_in = tokens.astype(jnp.float32)
    normed_one, inverse_one, pre_one = norm_forward(resid_in, gain_first, shift_first)
    hidden_one = pre_one.astype(jnp.bfloat16)
    projected = jnp.einsum(
        "rd,tdc->trc", hidden_one, attn_input, preferred_element_type=jnp.float32
    )
    queries = (projected[0] + query_bias).astype(jnp.bfloat16).reshape(row_count, -1, HD)
    keys_bf = projected[1].astype(jnp.bfloat16).reshape(row_count, -1, HD)
    values_bf = (projected[2] + value_bias).astype(jnp.bfloat16).reshape(row_count, -1, HD)
    mixed, log_sum = attend(queries, keys_bf, values_bf, allowed)
    attended = mixed.reshape(row_count, local_width).astype(jnp.bfloat16)
    attn_part = jnp.dot(attended, attn_output, preferred_element_type=jnp.float32)
    middle = resid_in + lax.psum(attn_part, "tensor") + output_bias
    normed_two, inverse_two, pre_two = norm_forward(middle, gain_second, shift_second)
    hidden_two = pre_two.astype(jnp.bfloat16)
    pre_act = jnp.dot(hidden_two, hidden_weight, preferred_element_type=jnp.float32) + hidden_bias
    gelu_value, gelu_slope = gelu_pair(pre_act)
    activation = gelu_value.astype(jnp.bfloat16)
    mlp_part = jnp.dot(activation, down_weight, preferred_element_type=jnp.float32)
    out_full = middle + lax.psum(mlp_part, "tensor") + down_bias
    block_out = jnp.where(valid, out_full, jnp.zeros_like(out_full)).astype(jnp.bfloat16)
    grad_top = cot_masked.astype(jnp.float32)
    grad_down_bias = jnp.sum(grad_top, axis=0)
    grad_down_weight = contract_rows(activation, cot_masked)
    grad_pre = contract_cols(cot_masked, down_weight) * gelu_slope
    grad_hidden_bias = jnp.sum(grad_pre, axis=0)
    grad_pre_bf = grad_pre.astype(jnp.bfloat16)
    grad_hidden_weight = contract_rows(hidden_two, grad_pre_bf)
    grad_two = lax.psum(contract_cols(grad_pre_bf, hidden_weight), "tensor")
    grad_gain_second = jnp.sum(grad_two * normed_two, axis=0)
    grad_shift_second = jnp.sum(grad_two, axis=0)
    grad_middle = grad_top + norm_backward(grad_two, normed_two, inverse_two, gain_second)
    grad_output_bias = jnp.sum(grad_middle, axis=0)
    grad_middle_bf = grad_middle.astype(jnp.bfloat16)
    grad_attn_output = contract_rows(attended, grad_middle_bf)
    grad_attended = (
        contract_cols(grad_middle_bf, attn_output).astype(jnp.bfloat16).reshape(row_count, -1, HD)
    )
    grad_queries, grad_keys, grad_values = attend_back(
        queries, keys_bf, values_bf, allowed, log_sum, grad_attended
    )
    grad_queries = grad_queries.reshape(row_count, local_width)
    grad_keys = grad_keys.reshape(row_count, local_width)
    grad_values = grad_values.reshape(row_count, local_width)
    grad_query_bias = jnp.sum(grad_queries, axis=0)
    grad_value_bias = jnp.sum(grad_values, axis=0)
    grad_stack = jnp.stack([grad_queries, grad_keys, grad_values]).astype(jnp.bfloat16)
    grad_attn_input = jnp.einsum(
        "rd,trc->tdc", hidden_one, grad_stack, preferred_element_type=jnp.float32
    )
    one_part = jnp.einsum("trc,tdc->rd", grad_stack, attn_input, preferred_element_type=jnp.float32)
    grad_one = lax.psum(one_part, "tensor")
    grad_gain_first = jnp.sum(grad_one * normed_one, axis=0)
    grad_shift_first = jnp.sum(grad_one, axis=0)
    input_grad = (
        grad_middle + norm_backward(grad_one, normed_one, inverse_one, gain_first)
    ).astype(jnp.bfloat16)
    (
        grad_attn_input,
        grad_query_bias,
        grad_value_bias,
        grad_attn_output,
        grad_output_bias,
        grad_gain_first,
        grad_shift_first,
        grad_hidden_weight,
        grad_hidden_bias,
        grad_down_weight,
        grad_down_bias,
        grad_gain_second,
        grad_shift_second,
    ) = lax.psum(
        (
            grad_attn_input,
            grad_query_bias,
            grad_value_bias,
            grad_attn_output,
            grad_output_bias,
            grad_gain_first,
            grad_shift_first,
            grad_hidden_weight,
            grad_hidden_bias,
            grad_down_weight,
            grad_down_bias,
            grad_gain_second,
            grad_shift_second,
        ),
        "dp",
    )
    return (
        block_out,
        input_grad,
        grad_attn_input,
        grad_query_bias,
        grad_value_bias,
        grad_attn_output,
        grad_output_bias,
        grad_gain_first,
        grad_shift_first,
        grad_hidden_weight,
        grad_hidden_bias,
        grad_down_weight,
        grad_down_bias,
        grad_gain_second,
        grad_shift_second,
    )


def shards(
    tokens,
    segment_ids,
    cotangent,
    attn_input,
    query_bias,
    value_bias,
    attn_output,
    output_bias,
    gain_first,
    shift_first,
    hidden_weight,
    hidden_bias,
    down_weight,
    down_bias,
    gain_second,
    shift_second,
):
    if lax.axis_size("tensor") != 4 or lax.axis_size("dp") != 8:
        return plain_shards(
            tokens,
            segment_ids,
            cotangent,
            attn_input,
            query_bias,
            value_bias,
            attn_output,
            output_bias,
            gain_first,
            shift_first,
            hidden_weight,
            hidden_bias,
            down_weight,
            down_bias,
            gain_second,
            shift_second,
        )
    local_width = attn_input.shape[2]
    width = tokens.shape[1]
    operands = (
        tokens,
        cotangent,
        segment_ids,
        attn_input.transpose(0, 2, 1).reshape(3 * local_width, width),
        query_bias,
        value_bias,
        attn_output,
        output_bias,
        gain_first,
        shift_first,
        hidden_weight,
        hidden_bias,
        down_weight,
        down_bias,
        gain_second,
        shift_second,
    )
    (
        block_out,
        input_grad,
        grad_in,
        grad_attn_output,
        grad_hidden_weight,
        grad_down_weight,
        grad_query_bias,
        grad_value_bias,
        grad_output_bias,
        grad_gain_first,
        grad_shift_first,
        grad_hidden_bias,
        grad_down_bias,
        grad_gain_second,
        grad_shift_second,
    ) = whole_block(operands)
    return (
        block_out,
        input_grad,
        grad_in.reshape(3, local_width, width).transpose(0, 2, 1),
        grad_query_bias,
        grad_value_bias,
        grad_attn_output,
        grad_output_bias,
        grad_gain_first,
        grad_shift_first,
        grad_hidden_weight,
        grad_hidden_bias,
        grad_down_weight,
        grad_down_bias,
        grad_gain_second,
        grad_shift_second,
    )


def solution(mesh):
    return jax.shard_map(
        shards,
        mesh=mesh,
        in_specs=(
            P("dp", None),
            P("dp"),
            P("dp", None),
            P(None, None, "tensor"),
            P("tensor"),
            P("tensor"),
            P("tensor", None),
            P(),
            P(),
            P(),
            P(None, "tensor"),
            P("tensor"),
            P("tensor", None),
            P(),
            P(),
            P(),
        ),
        out_specs=(
            P("dp", None),
            P("dp", None),
            P(None, None, "tensor"),
            P("tensor"),
            P("tensor"),
            P("tensor", None),
            P(),
            P(),
            P(),
            P(None, "tensor"),
            P("tensor"),
            P("tensor", None),
            P(),
            P(),
            P(),
        ),
        check_vma=False,
    )
```
